128 devices in a mesh: dp: 4 (over x), tm: 32 (over z, y, core).
Axes of the slice: x: 4, y: 4, z: 4, core: 2. Of those that a mesh axis runs over, the one named last changes fastest.
Arguments:
- clips: bfloat16 [4, 512, 512, 512], P('dp', 'tm'), may hold values from -6 to 6
- w_time: bfloat16 [3, 512, 512], P(None, 'dp'), may hold values from -0.15625 to 0.15625
- gain: float32 [512], replicated, may hold values from 0.1 to 1.9
- rate: float32 [512], replicated, may hold values from 9.765625e-05 to 0.0333333333
- keep: float32 [512], P('tm'), may hold values from 0.5 to 1
- latent_ids: int32 [512], P('tm'), may hold values from 0 to 63, as said below
- w_lat: bfloat16 [512, 16], replicated, may hold values from -0.25 to 0.25
Outputs:
- features: bfloat16 [4, 512, 512, 512], P('dp', 'tm')
- latents: float32 [4, 64, 16, 512], P('dp', 'tm')
The draws below stay inside these ranges and needn't reach their ends.
Inputs may be any that keep to these rules, and one draw needn't show every extreme that they name: latent_ids never falls as the frame grows; latent frame j begins at a frame from j * 8 - 7 to j * 8 (latent 0 at frame 0) and ends where the next begins; every latent frame gets 1 to 15 frames and the last exactly 15.
All inputs are finite; a program needn't handle non-finite values.
Results may differ from the reference program's by a relative error of at most 0.0025.
Values may be sent and summed in bfloat16 or wider, within the bound.
No kernel may reach another device: no remote copies, remote signals or barrier semaphores. Data moves between devices by JAX's collectives and lax.ppermute only.
A program may use at most 192 MiB of HBM per device.

```python
import math
import jax
import jax.numpy as jnp
from jax import lax

C = 512
LATC = 16
KT = 3
STRIDE = 8
P_SIZE = 512
VIDEO_LENGTH = 512
CLIPS = 4
LAT = 64


def draw_rate(key, part):
    first, second, final_portion = jax.random.split(key, 3)
    order = jax.random.permutation(first, C)
    fast_count = C // 2
    edge_markers = jnp.zeros((C,), jnp.float32).at[order[:fast_count]].set(1.0)
    fast = jax.random.uniform(second, (C,), jnp.float32, 1.0 / 50.0, 1.0 / 30.0)
    slow = jnp.exp(jax.random.uniform(final_portion, (C,), jnp.float32, math.log(0.05 / VIDEO_LENGTH), math.log(1.0 / VIDEO_LENGTH)))
    return edge_markers * fast + (1.0 - edge_markers) * slow


def draw_keep(key, part):
    first, second, final_portion = jax.random.split(key, 3)
    initial_displacement = jax.random.uniform(first, (VIDEO_LENGTH,), jnp.float32, 0.97, 1.0)
    order = jax.random.permutation(second, VIDEO_LENGTH)
    edge_markers = jnp.zeros((VIDEO_LENGTH,), jnp.float32).at[order[:3]].set(1.0)
    group_images = jax.random.uniform(final_portion, (VIDEO_LENGTH,), jnp.float32, 0.5, 0.8)
    return edge_markers * group_images + (1.0 - edge_markers) * initial_displacement


def draw_latent_ids(key, part):
    offsets = jax.random.randint(jax.random.fold_in(key, 11), (LAT,), 0, STRIDE).astype(jnp.int32)
    offsets = offsets.at[0].set(0).at[LAT - 1].set(STRIDE - 1)
    segment_starts = jnp.arange(LAT, dtype=jnp.int32) * STRIDE - offsets
    frames = jnp.arange(VIDEO_LENGTH, dtype=jnp.int32)
    return jnp.sum((frames[:, None] >= segment_starts[None, 1:]).astype(jnp.int32), 1).astype(jnp.int32)


def level_of(own_key, dims, cuts, smallest, high):
    loudness, own = 1.0, jax.random.fold_in(own_key, 6)
    for axis_at, parts in cuts:
        steps = jnp.exp(jax.random.uniform(jax.random.fold_in(own, axis_at), (parts,), jnp.float32, smallest / len(cuts), high / len(cuts)))
        loudness = loudness * jnp.repeat(steps, dims[axis_at] // parts).reshape([-1 if axis == axis_at else 1 for axis in range(len(dims))])
    return loudness


def centred(own_key, dims, spread, reach, cuts=(), held_as=jnp.bfloat16):
    result = jax.random.normal(own_key, dims, jnp.float32) * spread
    if len(cuts) > 0:
        result = level_of(own_key, dims, cuts, -0.22, 0.18) * result
    return jnp.clip(result, min=-reach, max=reach).astype(held_as)


def setup_inputs(seed: int = 0) -> dict:
    key_list = jax.random.split(jax.random.key(seed), 8)
    clips = centred(key_list[0], (CLIPS, VIDEO_LENGTH, P_SIZE, C), 1.0, 6.0, ((0, 4), (1, 32)))
    w_time = centred(key_list[1], (KT, C, C), (KT * C) ** -0.5, 0.15625, ((1, 4),))
    gain = jnp.clip(1.0 + 0.18 * jax.random.normal(key_list[2], (C,), jnp.float32), 0.1, 1.9)
    rate = draw_rate(jax.random.fold_in(key_list[7], 71), 0)
    keep = draw_keep(jax.random.fold_in(key_list[7], 71), 0)
    latent_ids = draw_latent_ids(jax.random.fold_in(key_list[7], 71), 0)
    w_lat = centred(key_list[6], (C, LATC), C ** -0.5, 0.25)
    return dict(clips=clips, w_time=w_time, gain=gain, rate=rate, keep=keep, latent_ids=latent_ids, w_lat=w_lat)


def causal_conv(clip, w_time):
    padded = jnp.concatenate([jnp.zeros((KT - 1,) + clip.shape[1:], clip.dtype), clip], 0)
    total = jnp.zeros((VIDEO_LENGTH * P_SIZE, C), jnp.float32)
    for k in range(KT):
        part = padded[KT - 1 - k:KT - 1 - k + VIDEO_LENGTH].reshape(VIDEO_LENGTH * P_SIZE, C)
        total = total + jnp.dot(part, w_time[k], preferred_element_type=jnp.float32)
    return total.reshape(VIDEO_LENGTH, P_SIZE, C)

def reference(clips, w_time, gain, rate, keep, latent_ids, w_lat):
    decay = jnp.exp(-rate)
    inject = jnp.sqrt(-jnp.expm1(-2.0 * rate))
    retain = decay[None, :] * keep[:, None]
    onehot = (latent_ids[:, None] == jnp.arange(LAT, dtype=jnp.int32)[None, :]).astype(jnp.float32)
    counts = lax.optimization_barrier(jnp.sum(onehot, 0))

    def one_clip(clip):
        conv = causal_conv(clip, w_time)
        features = (clip.astype(jnp.float32) + jax.nn.silu(conv)).astype(jnp.bfloat16)
        values = features.astype(jnp.float32)
        normed = values * lax.rsqrt(lax.optimization_barrier(jnp.mean(values * values, -1, keepdims=True)) + 1e-06) * gain

        def step(state, inputs):
            kept, entry = inputs
            state = kept[None, :] * state + inject[None, :] * entry
            return (state, state)
        _, state = lax.scan(step, jnp.zeros((P_SIZE, C), jnp.float32), (retain, normed))
        state_b = state.astype(jnp.bfloat16)
        proj = jnp.dot(state_b.reshape(VIDEO_LENGTH * P_SIZE, C), w_lat, preferred_element_type=jnp.float32)
        proj = jnp.transpose(proj.reshape(VIDEO_LENGTH, P_SIZE, LATC), (0, 2, 1))
        sums = jnp.einsum('fj,flp->jlp', onehot, proj, precision=lax.Precision.HIGHEST)
        return (features, sums / counts[:, None, None])
    features, latents = lax.map(one_clip, clips)
    return (features, latents)
```

```python
import functools

import jax
import jax.numpy as jnp
from jax import lax
from jax.experimental import pallas as pl
from jax.experimental.pallas import tpu as pltpu
from jax.sharding import PartitionSpec as P

KT = 3
STRIDE = 8
F32 = jnp.float32
BF16 = jnp.bfloat16
CHUNKS = (256, 256)
SUB = 16


def rotated(value, axis, steps):
    count = lax.axis_size(axis)
    return lax.ppermute(value, axis, [(s, (s + steps) % count) for s in range(count)])


def shifted(value, axis, steps):
    count = lax.axis_size(axis)
    return lax.ppermute(value, axis, [(s, s + steps) for s in range(count - steps)])


def swapped(value, axis):
    return lax.ppermute(value, axis, [(s, s ^ 1) for s in range(lax.axis_size(axis))])


def conv_kernel(window, keep, x_hbm, halo_hbm, own, da, db, dc, sa, sb, sc, decay, *rest, start, width, shards):
    feat_hbm, last, pooled, w, X, H, F, wsem, insem, outsem = rest[-10:]
    nframe = x_hbm.shape[0]
    half = da.shape[1]
    depth = own.shape[1]
    me = lax.axis_index("dp")
    side = lax.rem(lax.axis_index("tm"), 2)

    def weights():
        copies = [pltpu.make_async_copy(own, w.at[:, pl.ds(pl.multiple_of(me * depth, depth), depth)], wsem.at[0])]
        slot = 1
        for step, mine, other in ((shards - 1, da, sa), (1, db, sb), (2, dc, sc)):
            base = lax.rem(me + step, shards) * depth
            for piece, lane in ((mine, side), (other, 1 - side)):
                row = pl.multiple_of(base + lane * half, half)
                copies.append(pltpu.make_async_copy(piece, w.at[:, pl.ds(row, half)], wsem.at[slot]))
                slot += 1
        return copies

    def prior(f):
        return pltpu.make_async_copy(halo_hbm.at[f, pl.ds(start, width)], X.at[f], insem.at[f])

    def entering(f):
        return pltpu.make_async_copy(x_hbm.at[f, pl.ds(start, width)], X.at[f + KT - 1], insem.at[f + KT - 1])

    def leaving(f, slot):
        return pltpu.make_async_copy(F.at[slot], feat_hbm.at[f, pl.ds(start, width)], outsem.at[slot])

    def product(f, slot):
        nchan = w.shape[2]
        for n in range(0, nchan, 256):
            total = None
            for k in range(KT):
                part = jnp.dot(X[f + KT - 1 - k], w[k, :, n : n + 256], preferred_element_type=F32)
                total = part if total is None else total + part
            H[slot, :, n : n + 256] = total

    def finish(f, slot):
        j = window[f]
        kept = decay[...] * keep[f]
        nchan = w.shape[2]
        for r in range(0, width, SUB):
            h = H[slot, r : r + SUB, :]
            c = X[f + KT - 1, r : r + SUB, :].astype(F32)
            rounded = (c + (h + h * jnp.tanh(h))).astype(BF16)
            F[slot, r : r + SUB, :] = rounded
            v = rounded.astype(F32)
            scale = lax.rsqrt(jnp.sum(v * v, -1, keepdims=True) * (1.0 / nchan) + 1e-06)
            state = last[r : r + SUB, :] * kept + v * scale
            last[r : r + SUB, :] = state
            pooled[j, r : r + SUB, :] += state

    pieces = weights()
    for copy in pieces:
        copy.start()
    for f in range(KT - 1):
        prior(f).start()
    for f in range(nframe):
        entering(f).start()
    last[...] = jnp.zeros_like(last)
    pooled[...] = jnp.zeros_like(pooled)
    for copy in pieces:
        copy.wait()
    for f in range(KT - 1):
        prior(f).wait()
    entering(0).wait()
    product(0, 0)

    def body(f, _):
        slot = lax.rem(f, 2)

        @pl.when(f >= 2)
        def _():
            leaving(f - 2, slot).wait()

        entering(f + 1).wait()
        product(f + 1, 1 - slot)
        finish(f, slot)
        leaving(f, slot).start()
        return 0

    lax.fori_loop(0, nframe - 1, body, 0)
    final = (nframe - 1) % 2
    leaving(nframe - 3, final).wait()
    finish(nframe - 1, final)
    leaving(nframe - 1, final).start()
    leaving(nframe - 2, 1 - final).wait()
    leaving(nframe - 1, final).wait()


def table_kernel(keep, ids, rate, scaled, high, low, E):
    nall = keep.shape[1]
    nchan = rate.shape[1]
    nlat = high.shape[0]
    end = (lax.axis_index("tm") + 1) * (nall // lax.axis_size("tm")) - 1
    logs = jnp.log(keep[...])
    block = 128
    for r in range(0, nall, block):
        rows = lax.broadcasted_iota(jnp.int32, (block, nall), 0) + r
        cols = lax.broadcasted_iota(jnp.int32, (block, nall), 1)
        between = jnp.logical_and(cols > end, cols <= rows)
        run = jnp.sum(jnp.where(between, logs, 0.0), -1, keepdims=True)
        frame = lax.broadcasted_iota(jnp.int32, (block, nchan), 0) + r
        gap = (frame - end).astype(F32)
        E[r : r + block, :] = jnp.where(frame > end, jnp.exp(run - rate[...] * gap), 0.0)
    member = lax.broadcasted_iota(jnp.int32, (nlat, nall), 0) == ids[...]
    table = jnp.dot(member.astype(F32), E[...], precision=lax.Precision.HIGHEST, preferred_element_type=F32)
    E[0:nlat, :] = table
    for j in range(nlat):
        value = scaled[...] * E[j : j + 1, :]
        upper = value.astype(BF16)
        high[j] = upper
        low[j] = (value - upper.astype(F32)).astype(BF16)


def times(a, b):
    return lax.dot_general(a, b, (((1,), (1,)), ((), ())), preferred_element_type=F32)


def split(value):
    upper = value.astype(BF16)
    return upper, (value - upper.astype(F32)).astype(BF16)


def spread_kernel(high, low, scaled, last, pooled, sends, own):
    nlat, nproj, nchan = high.shape
    ndev = sends.shape[0]
    width = last.shape[0]
    top, rest = split(last[...])
    rows = 256
    per = sends.shape[1]
    for r in range(0, nlat * nproj, rows):
        upper = high[r // nproj : (r + rows) // nproj].reshape(rows, nchan)
        lower = low[r // nproj : (r + rows) // nproj].reshape(rows, nchan)
        z = times(upper, top) + times(upper, rest) + times(lower, top)
        sends[r // per : (r + rows) // per] = z.reshape(rows // per, per, width).astype(BF16)
    upper, lower = split(scaled[...])
    parts = []
    for j in range(3):
        top, rest = split(pooled[j])
        parts.append(times(upper, top) + times(upper, rest) + times(lower, top))
    own[0:nproj, :] = parts[0]
    own[nproj : 2 * nproj, :] = parts[1]
    me = lax.axis_index("tm")

    @pl.when(me < ndev - 1)
    def _():
        block = sends[me + 1]
        sends[me + 1, 0:nproj] = (block[0:nproj].astype(F32) + parts[2]).astype(BF16)


def per_device(clips, w_time, gain, rate, keep, latent_ids, w_lat):
    nclip, nframe, npos, nchan = clips.shape
    nproj = w_lat.shape[1]
    ndev = lax.axis_size("tm")
    shards = lax.axis_size("dp")
    nall = nframe * ndev
    per = nframe // STRIDE
    nlat = per * ndev
    me = lax.axis_index("tm")
    side = me % 2
    x = clips[0]

    own_w = w_time * jnp.asarray(0.5, BF16)
    half = own_w.shape[1] // 2
    mine = lax.dynamic_slice_in_dim(own_w, side * half, half, 1)
    halo = shifted(x[nframe - (KT - 1) :], "tm", 1)
    da, db, dc = rotated(mine, "dp", 1), rotated(mine, "dp", -1), rotated(mine, "dp", 2)
    sa, sb, sc = swapped(da, "tm"), swapped(db, "tm"), swapped(dc, "tm")

    local = jnp.stack([keep, latent_ids.astype(F32)])[None]
    seen = local
    step = 1
    while step < ndev:
        seen = jnp.concatenate([seen, rotated(seen, "tm", -step)], 0)
        step *= 2
    seen = jnp.roll(seen, me, 0)
    seen = jnp.moveaxis(seen, 1, 0).reshape(2, nall)
    keep_all = seen[0:1]
    ids_all = seen[1:2].astype(jnp.int32)

    decay = jnp.exp(-rate)[None]
    inject = jnp.sqrt(-jnp.expm1(-2.0 * rate))
    scaled = w_lat.T.astype(F32) * (inject * gain)[None]

    vmem = pl.BlockSpec(memory_space=pltpu.VMEM)
    smem = pl.BlockSpec(memory_space=pltpu.SMEM)
    hbm = pl.BlockSpec(memory_space=pl.ANY)
    table_shape = jax.ShapeDtypeStruct((nlat, nproj, nchan), BF16)
    high, low = pl.pallas_call(
        table_kernel,
        out_shape=(table_shape, table_shape),
        in_specs=[vmem] * 4,
        out_specs=(vmem, vmem),
        scratch_shapes=[pltpu.VMEM((nall, nchan), F32)],
        compiler_params=pltpu.CompilerParams(vmem_limit_bytes=24 << 20),
        cost_estimate=pl.CostEstimate(flops=6 * nlat * nall * nchan, bytes_accessed=4 << 20, transcendentals=nall * nchan),
        name="tables",
    )(keep_all, ids_all, rate[None], scaled)

    window = latent_ids - me.astype(jnp.int32) * per
    features = None
    start = 0
    outs = []
    for index, width in enumerate(CHUNKS):
        before = () if features is None else (features,)
        features, last, pooled = pl.pallas_call(
            functools.partial(conv_kernel, start=start, width=width, shards=shards),
            out_shape=(
                jax.ShapeDtypeStruct((nframe, npos, nchan), BF16),
                jax.ShapeDtypeStruct((width, nchan), F32),
                jax.ShapeDtypeStruct((3, width, nchan), F32),
            ),
            in_specs=[smem, smem] + [hbm] * 9 + [vmem] + [hbm] * len(before),
            out_specs=(hbm, vmem, vmem),
            input_output_aliases={12: 0} if before else {},
            scratch_shapes=[
                pltpu.VMEM((KT, nchan, nchan), BF16),
                pltpu.VMEM((nframe + KT - 1, width, nchan), BF16),
                pltpu.VMEM((2, width, nchan), F32),
                pltpu.VMEM((2, width, nchan), BF16),
                pltpu.SemaphoreType.DMA((7,)),
                pltpu.SemaphoreType.DMA((nframe + KT - 1,)),
                pltpu.SemaphoreType.DMA((2,)),
            ],
            compiler_params=pltpu.CompilerParams(vmem_limit_bytes=24 << 20),
            cost_estimate=pl.CostEstimate(
                flops=2 * KT * nframe * width * nchan * nchan,
                bytes_accessed=4 * nframe * width * nchan,
                transcendentals=nframe * width * nchan,
            ),
            name=f"conv{index}",
        )(window, keep, x, halo, own_w, da, db, dc, sa, sb, sc, decay, *before)
        sends, own = pl.pallas_call(
            spread_kernel,
            out_shape=(
                jax.ShapeDtypeStruct((ndev, per * nproj, width), BF16),
                jax.ShapeDtypeStruct((per * nproj, width), F32),
            ),
            in_specs=[vmem] * 5,
            out_specs=(vmem, vmem),
            compiler_params=pltpu.CompilerParams(vmem_limit_bytes=24 << 20),
            cost_estimate=pl.CostEstimate(
                flops=6 * nlat * nproj * nchan * width, bytes_accessed=8 << 20, transcendentals=0
            ),
            name=f"spread{index}",
        )(high, low, scaled, last, pooled)
        got = lax.all_to_all(sends, "tm", 0, 0)
        outs.append((got, own))
        start += width

    mine_ids = me * per + jnp.arange(per, dtype=jnp.int32)
    counts = jnp.sum((ids_all == mine_ids[:, None]).astype(F32), 1)
    latents = []
    for got, own in outs:
        total = own + jnp.sum(got.astype(F32), 0)
        latents.append(total.reshape(per, nproj, -1) / counts[:, None, None])
    return features[None], jnp.concatenate(latents, -1)[None]


def solution(mesh):
    return jax.shard_map(
        per_device,
        mesh=mesh,
        in_specs=(P("dp", "tm", None, None), P(None, "dp", None), P(), P(), P("tm"), P("tm"), P()),
        out_specs=(P("dp", "tm", None, None), P("dp", "tm", None, None)),
        check_vma=False,
    )
```

```python
import functools

import jax
import jax.numpy as jnp
from jax import lax
from jax.experimental import pallas as pl
from jax.experimental.pallas import tpu as pltpu
from jax.sharding import PartitionSpec as P


KT = 3
STRIDE = 8
F32 = jnp.float32
BF16 = jnp.bfloat16
CHUNKS = (256, 256)
SUB = 16


def rotated(value, axis, steps):
    count = lax.axis_size(axis)
    return lax.ppermute(value, axis, [(s, (s + steps) % count) for s in range(count)])


def shifted(value, axis, steps):
    count = lax.axis_size(axis)
    return lax.ppermute(value, axis, [(s, s + steps) for s in range(count - steps)])


def swapped(value, axis):
    return lax.ppermute(value, axis, [(s, s ^ 1) for s in range(lax.axis_size(axis))])


def conv_kernel(window, keep, x_hbm, halo_hbm, own, da, db, dc, sa, sb, sc, decay, *rest, start, width, shards):
    feat_hbm, last, pooled, w, X, H, F, wsem, insem, outsem = rest[-10:]
    nframe = x_hbm.shape[0]
    half = da.shape[1]
    depth = own.shape[1]
    me = lax.axis_index("dp")
    side = lax.rem(lax.axis_index("tm"), 2)

    def weights():
        copies = [pltpu.make_async_copy(own, w.at[:, pl.ds(pl.multiple_of(me * depth, depth), depth)], wsem.at[0])]
        slot = 1
        for step, mine, other in ((shards - 1, da, sa), (1, db, sb), (2, dc, sc)):
            base = lax.rem(me + step, shards) * depth
            for piece, lane in ((mine, side), (other, 1 - side)):
                row = pl.multiple_of(base + lane * half, half)
                copies.append(pltpu.make_async_copy(piece, w.at[:, pl.ds(row, half)], wsem.at[slot]))
                slot += 1
        return copies

    def prior(f):
        return pltpu.make_async_copy(halo_hbm.at[f, pl.ds(start, width)], X.at[f], insem.at[f])

    def entering(f):
        return pltpu.make_async_copy(x_hbm.at[f, pl.ds(start, width)], X.at[f + KT - 1], insem.at[f + KT - 1])

    def leaving(f, slot):
        return pltpu.make_async_copy(F.at[slot], feat_hbm.at[f, pl.ds(start, width)], outsem.at[slot])

    def product(f, slot):
        nchan = w.shape[2]
        for n in range(0, nchan, 256):
            total = None
            for k in range(KT):
                part = jnp.dot(X[f + KT - 1 - k], w[k, :, n : n + 256], preferred_element_type=F32)
                total = part if total is None else total + part
            H[slot, :, n : n + 256] = total

    def finish(f, slot):
        j = window[f]
        kept = decay[...] * keep[f]
        nchan = w.shape[2]
        for r in range(0, width, SUB):
            h = H[slot, r : r + SUB, :]
            c = X[f + KT - 1, r : r + SUB, :].astype(F32)
            rounded = (c + (h + h * jnp.tanh(h))).astype(BF16)
            F[slot, r : r + SUB, :] = rounded
            v = rounded.astype(F32)
            scale = lax.rsqrt(jnp.sum(v * v, -1, keepdims=True) * (1.0 / nchan) + 1e-06)
            state = last[r : r + SUB, :] * kept + v * scale
            last[r : r + SUB, :] = state
            pooled[j, r : r + SUB, :] += state

    pieces = weights()
    for copy in pieces:
        copy.start()
    for f in range(KT - 1):
        prior(f).start()
    for f in range(nframe):
        entering(f).start()
    last[...] = jnp.zeros_like(last)
    pooled[...] = jnp.zeros_like(pooled)
    for copy in pieces:
        copy.wait()
    for f in range(KT - 1):
        prior(f).wait()
    entering(0).wait()
    product(0, 0)

    def body(f, _):
        slot = lax.rem(f, 2)

        @pl.when(f >= 2)
        def _():
            leaving(f - 2, slot).wait()

        entering(f + 1).wait()
        product(f + 1, 1 - slot)
        finish(f, slot)
        leaving(f, slot).start()
        return 0

    lax.fori_loop(0, nframe - 1, body, 0)
    final = (nframe - 1) % 2
    leaving(nframe - 3, final).wait()
    finish(nframe - 1, final)
    leaving(nframe - 1, final).start()
    leaving(nframe - 2, 1 - final).wait()
    leaving(nframe - 1, final).wait()


def table_kernel(packed, rate, scaled, high, low, counts, E):
    nall, lanes = packed.shape
    nchan = rate.shape[1]
    nlat = high.shape[0]
    me = lax.axis_index("tm")
    end = (me + 1) * (nall // lax.axis_size("tm")) - 1
    frame = lax.broadcasted_iota(jnp.int32, (nall, lanes), 0)
    logs = jnp.where(frame > end, jnp.log(jnp.maximum(packed[...], 0.5)), 0.0)
    rows = lax.broadcasted_iota(jnp.int32, (nall, nall), 0)
    cols = lax.broadcasted_iota(jnp.int32, (nall, nall), 1)
    run = jnp.dot(
        (cols <= rows).astype(F32), logs, precision=lax.Precision.HIGHEST, preferred_element_type=F32
    )
    block = 128
    for r in range(0, nall, block):
        at = lax.broadcasted_iota(jnp.int32, (block, nchan), 0) + r
        gap = (at - end).astype(F32)
        E[r : r + block, :] = jnp.where(at > end, jnp.exp(run[r : r + block, 0:1] - rate[...] * gap), 0.0)
    ids = packed[:, lanes // 2 : lanes // 2 + 1].astype(jnp.int32)
    member = (lax.broadcasted_iota(jnp.int32, (nall, lanes), 1) == ids).astype(F32)
    table = lax.dot_general(
        member, E[...], (((0,), (0,)), ((), ())), precision=lax.Precision.HIGHEST, preferred_element_type=F32
    )
    per = counts.shape[0]
    for i in range(per):
        hit = (jnp.broadcast_to(ids, (nall, lanes)) == me * per + i).astype(F32)
        counts[i : i + 1, :] = jnp.sum(hit, 0, keepdims=True)
    E[0:lanes, :] = table
    for j in range(nlat):
        value = scaled[...] * E[j : j + 1, :]
        upper = value.astype(BF16)
        high[j] = upper
        low[j] = (value - upper.astype(F32)).astype(BF16)


def times(a, b):
    return lax.dot_general(a, b, (((1,), (1,)), ((), ())), preferred_element_type=F32)


def split(value):
    upper = value.astype(BF16)
    return upper, (value - upper.astype(F32)).astype(BF16)


def spread_kernel(high, low, scaled, last, pooled, sends, own):
    nlat, nproj, nchan = high.shape
    ndev = sends.shape[0]
    width = last.shape[0]
    top, rest = split(last[...])
    rows = 256
    per = sends.shape[1]
    for r in range(0, nlat * nproj, rows):
        upper = high[r // nproj : (r + rows) // nproj].reshape(rows, nchan)
        lower = low[r // nproj : (r + rows) // nproj].reshape(rows, nchan)
        z = times(upper, top) + times(upper, rest) + times(lower, top)
        sends[r // per : (r + rows) // per] = z.reshape(rows // per, per, width).astype(BF16)
    upper, lower = split(scaled[...])
    parts = []
    for j in range(3):
        top, rest = split(pooled[j])
        parts.append(times(upper, top) + times(upper, rest) + times(lower, top))
    own[0:nproj, :] = parts[0]
    own[nproj : 2 * nproj, :] = parts[1]
    me = lax.axis_index("tm")

    @pl.when(me < ndev - 1)
    def _():
        block = sends[me + 1]
        sends[me + 1, 0:nproj] = (block[0:nproj].astype(F32) + parts[2]).astype(BF16)


def final_kernel(counts, *refs):
    per = counts.shape[0]
    latents = refs[-1]
    start = 0
    for index in range(len(refs) // 2):
        got, own = refs[2 * index], refs[2 * index + 1]
        ndev, rows, width = got.shape
        nproj = rows // per
        for i in range(per):
            part = slice(i * nproj, (i + 1) * nproj)
            total = own[part, :]
            for d in range(ndev):
                total = total + got[d, part, :].astype(F32)
            for n in range(0, width, 128):
                latents[i, :, start + n : start + n + 128] = total[:, n : n + 128] / counts[i : i + 1, :]
        start += width


def per_device(clips, w_time, gain, rate, keep, latent_ids, w_lat):
    _, nframe, npos, nchan = clips.shape
    nproj = w_lat.shape[1]
    ndev = lax.axis_size("tm")
    shards = lax.axis_size("dp")
    nall = nframe * ndev
    per = nframe // STRIDE
    nlat = per * ndev
    me = lax.axis_index("tm")
    side = me % 2
    x = clips[0]

    own_w = w_time * jnp.asarray(0.5, BF16)
    half = own_w.shape[1] // 2
    mine = lax.dynamic_slice_in_dim(own_w, side * half, half, 1)
    halo = shifted(x[nframe - (KT - 1) :], "tm", 1)
    da, db, dc = rotated(mine, "dp", 1), rotated(mine, "dp", -1), rotated(mine, "dp", 2)
    sa, sb, sc = swapped(da, "tm"), swapped(db, "tm"), swapped(dc, "tm")

    lane = jnp.arange(128, dtype=jnp.int32)[None]
    local = jnp.where(lane < 64, keep[:, None], latent_ids.astype(F32)[:, None])
    local = jnp.broadcast_to(local[None], (ndev, nframe, 128))
    packed = lax.all_to_all(local, "tm", 0, 0).reshape(nall, 128)

    decay = jnp.exp(-rate)[None]
    inject = jnp.sqrt(-jnp.expm1(-2.0 * rate))
    scaled = w_lat.T.astype(F32) * (inject * gain)[None]

    vmem = pl.BlockSpec(memory_space=pltpu.VMEM)
    smem = pl.BlockSpec(memory_space=pltpu.SMEM)
    hbm = pl.BlockSpec(memory_space=pltpu.HBM)
    table_shape = jax.ShapeDtypeStruct((nlat, nproj, nchan), BF16)

    window = latent_ids - me.astype(jnp.int32) * per
    features = None
    start = 0
    outs = []
    for index, width in enumerate(CHUNKS):
        before = () if features is None else (features,)
        conv = pl.pallas_call(
            functools.partial(conv_kernel, start=start, width=width, shards=shards),
            out_shape=(
                jax.ShapeDtypeStruct((nframe, npos, nchan), BF16),
                jax.ShapeDtypeStruct((width, nchan), F32),
                jax.ShapeDtypeStruct((3, width, nchan), F32),
            ),
            in_specs=[smem, smem] + [hbm] * 9 + [vmem] + [hbm] * len(before),
            out_specs=(hbm, vmem, vmem),
            input_output_aliases={12: 0} if before else {},
            scratch_shapes=[
                pltpu.VMEM((KT, nchan, nchan), BF16),
                pltpu.VMEM((nframe + KT - 1, width, nchan), BF16),
                pltpu.VMEM((2, width, nchan), F32),
                pltpu.VMEM((2, width, nchan), BF16),
                pltpu.SemaphoreType.DMA((7,)),
                pltpu.SemaphoreType.DMA((nframe + KT - 1,)),
                pltpu.SemaphoreType.DMA((2,)),
            ],
            cost_estimate=pl.CostEstimate(
                flops=2 * KT * nframe * width * nchan * nchan,
                bytes_accessed=4 * nframe * width * nchan,
                transcendentals=nframe * width * nchan,
            ),
        )
        features, last, pooled = conv(window, keep, x, halo, own_w, da, db, dc, sa, sb, sc, decay, *before)
        if index == 0:
            packed, last = lax.optimization_barrier((packed, last))
            high, low, counts = pl.pallas_call(
                table_kernel,
                out_shape=(table_shape, table_shape, jax.ShapeDtypeStruct((per, 128), F32)),
                in_specs=[vmem] * 3,
                out_specs=(vmem,) * 3,
                scratch_shapes=[pltpu.VMEM((nall, nchan), F32)],
                compiler_params=pltpu.CompilerParams(vmem_limit_bytes=24 << 20),
                cost_estimate=pl.CostEstimate(
                    flops=12 * nlat * nall * nchan, bytes_accessed=4 << 20, transcendentals=nall * nchan
                ),
                name="tables",
            )(packed, rate[None], scaled)
        sends, own = pl.pallas_call(
            spread_kernel,
            out_shape=(
                jax.ShapeDtypeStruct((ndev, per * nproj, width), BF16),
                jax.ShapeDtypeStruct((per * nproj, width), F32),
            ),
            in_specs=[vmem] * 5,
            out_specs=(vmem, vmem),
            compiler_params=pltpu.CompilerParams(vmem_limit_bytes=24 << 20),
            cost_estimate=pl.CostEstimate(
                flops=6 * nlat * nproj * nchan * width, bytes_accessed=8 << 20, transcendentals=0
            ),
        )(high, low, scaled, last, pooled)
        if index < len(CHUNKS) - 1:
            features, sends = lax.optimization_barrier((features, sends))
        outs += [lax.all_to_all(sends, "tm", 0, 0), own]
        start += width

    latents = pl.pallas_call(
        final_kernel,
        out_shape=jax.ShapeDtypeStruct((per, nproj, npos), F32),
        in_specs=[vmem] * (1 + len(outs)),
        out_specs=vmem,
        compiler_params=pltpu.CompilerParams(vmem_limit_bytes=16 << 20),
        name="final",
    )(counts, *outs)
    return features[None], latents[None]


def solution(mesh):
    return jax.shard_map(
        per_device,
        mesh=mesh,
        in_specs=(P("dp", "tm", None, None), P(None, "dp", None), P(), P(), P("tm"), P("tm"), P()),
        out_specs=(P("dp", "tm", None, None), P("dp", "tm", None, None)),
        check_vma=False,
    )
```

```python
import functools

import jax
import jax.numpy as jnp
from jax import lax
from jax.experimental import pallas as pl
from jax.experimental.pallas import tpu as pltpu
from jax.sharding import PartitionSpec as P


KT = 3
STRIDE = 8
F32 = jnp.float32
BF16 = jnp.bfloat16
TILE = 128
GROUP = 4
ROWS = 256
SUB = 16


def rotated(value, axis, steps):
    count = lax.axis_size(axis)
    return lax.ppermute(value, axis, [(s, (s + steps) % count) for s in range(count)])


def shifted(value, axis, steps):
    count = lax.axis_size(axis)
    return lax.ppermute(value, axis, [(s, s + steps) for s in range(count - steps)])


def swapped(value, axis):
    return lax.ppermute(value, axis, [(s, s ^ 1) for s in range(lax.axis_size(axis))])


def table_kernel(packed, rate, scaled, high, low, counts, E):
    nall, lanes = packed.shape
    nchan = rate.shape[1]
    nlat = high.shape[0]
    me = lax.axis_index("tm")
    end = (me + 1) * (nall // lax.axis_size("tm")) - 1
    frame = lax.broadcasted_iota(jnp.int32, (nall, lanes), 0)
    logs = jnp.where(frame > end, jnp.log(jnp.maximum(packed[...], 0.5)), 0.0)
    rows = lax.broadcasted_iota(jnp.int32, (nall, nall), 0)
    cols = lax.broadcasted_iota(jnp.int32, (nall, nall), 1)
    run = jnp.dot(
        (cols <= rows).astype(F32), logs, precision=lax.Precision.HIGHEST, preferred_element_type=F32
    )
    block = 128
    for r in range(0, nall, block):
        at = lax.broadcasted_iota(jnp.int32, (block, nchan), 0) + r
        gap = (at - end).astype(F32)
        E[r : r + block, :] = jnp.where(at > end, jnp.exp(run[r : r + block, 0:1] - rate[...] * gap), 0.0)
    ids = packed[:, lanes // 2 : lanes // 2 + 1].astype(jnp.int32)
    member = (lax.broadcasted_iota(jnp.int32, (nall, lanes), 1) == ids).astype(F32)
    table = lax.dot_general(
        member, E[...], (((0,), (0,)), ((), ())), precision=lax.Precision.HIGHEST, preferred_element_type=F32
    )
    per = counts.shape[0]
    for i in range(per):
        hit = (jnp.broadcast_to(ids, (nall, lanes)) == me * per + i).astype(F32)
        counts[i : i + 1, :] = jnp.sum(hit, 0, keepdims=True)
    E[0:lanes, :] = table
    for j in range(nlat):
        value = scaled[...] * E[j : j + 1, :]
        upper = value.astype(BF16)
        high[j] = upper
        low[j] = (value - upper.astype(F32)).astype(BF16)


def times(a, b):
    return lax.dot_general(a, b, (((1,), (1,)), ((), ())), preferred_element_type=F32)


def split(value):
    upper = value.astype(BF16)
    return upper, (value - upper.astype(F32)).astype(BF16)


def spread(high, low, scaled, last, pooled, sends, own):
    nlat, nproj, nchan = high.shape
    ndev = sends.shape[0]
    width = last.shape[0]
    top, rest = split(last[...])
    rows = 256
    per = sends.shape[1]
    for r in range(0, nlat * nproj, rows):
        upper = high[r // nproj : (r + rows) // nproj].reshape(rows, nchan)
        lower = low[r // nproj : (r + rows) // nproj].reshape(rows, nchan)
        z = times(upper, top) + times(upper, rest) + times(lower, top)
        sends[r // per : (r + rows) // per] = z.reshape(rows // per, per, width).astype(BF16)
    upper, lower = split(scaled[...])
    parts = []
    for j in range(3):
        top, rest = split(pooled[j])
        parts.append(times(upper, top) + times(upper, rest) + times(lower, top))
    own[0:nproj, :] = parts[0]
    own[nproj : 2 * nproj, :] = parts[1]
    me = lax.axis_index("tm")

    @pl.when(me < ndev - 1)
    def _():
        block = sends[me + 1]
        sends[me + 1, 0:nproj] = (block[0:nproj].astype(F32) + parts[2]).astype(BF16)


def conv_kernel(
    window, keep, x_hbm, halo_hbm, own_w, da, db, dc, sa, sb, sc, decay, high, low, scaled,
    feat_hbm, sends, own, w, X, HA, HB, FA, FB, R, last, pooled, wsem, insem, outsem, *, shards,
):
    nframe, npos, nchan = x_hbm.shape
    tiles, groups = npos // TILE, nframe // GROUP
    total = tiles * groups
    H, F = (HA, HB), (FA, FB)
    half, depth = da.shape[1], own_w.shape[1]
    me = lax.axis_index("dp")
    side = lax.rem(lax.axis_index("tm"), 2)
    lead = KT - 1

    def weights():
        copies = [pltpu.make_async_copy(own_w, w.at[:, pl.ds(pl.multiple_of(me * depth, depth), depth)], wsem.at[0])]
        slot = 1
        for step, mine, other in ((shards - 1, da, sa), (1, db, sb), (2, dc, sc)):
            base = lax.rem(me + step, shards) * depth
            for piece, lane in ((mine, side), (other, 1 - side)):
                row = pl.multiple_of(base + lane * half, half)
                copies.append(pltpu.make_async_copy(piece, w.at[:, pl.ds(row, half)], wsem.at[slot]))
                slot += 1
        return copies

    def entering(q):
        part = pl.ds(q * TILE, TILE)
        return pltpu.make_async_copy(x_hbm.at[:, part], X.at[lead : lead + nframe, part], insem.at[q])

    def prior(q):
        part = pl.ds(q * TILE, TILE)
        return pltpu.make_async_copy(halo_hbm.at[:, part], X.at[0:lead, part], insem.at[tiles + q])

    def place(i):
        return pl.multiple_of(i // groups * TILE, TILE), lax.rem(i, groups) * GROUP

    def leaving(i, s):
        p, f = place(i)
        return pltpu.make_async_copy(F[s], feat_hbm.at[pl.ds(f, GROUP), pl.ds(p, TILE)], outsem.at[s])

    def product(i, s, m, n):
        p, f = place(i)
        count = ROWS // TILE
        acc = None
        for k in range(KT):
            rows = X[pl.ds(f + lead - k + m * count, count), pl.ds(p, TILE), :].reshape(ROWS, nchan)
            part = jnp.dot(rows, w[k, :, n : n + 256], preferred_element_type=F32)
            acc = part if acc is None else acc + part
        H[s][m * ROWS : (m + 1) * ROWS, n : n + 256] = acc

    def activate(i, s, g, r):
        p, f = place(i)
        at = g * TILE + r
        h = H[s][at : at + SUB, :]
        c = X[f + lead + g, pl.ds(p + r, SUB), :].astype(F32)
        value = c + (h + h * jnp.tanh(h))
        F[s][g, r : r + SUB, :] = value.astype(BF16)
        mean = jnp.sum(value * value, -1, keepdims=True) * (1.0 / nchan)
        R[at : at + SUB, :] = jnp.broadcast_to(lax.rsqrt(mean + 1e-06), (SUB, 128))

    def recur(i, s, r):
        p, f = place(i)
        rows = pl.ds(p + r, SUB)
        state = last[rows, :]
        for g in range(GROUP):
            scale = R[g * TILE + r : g * TILE + r + SUB, :]
            v = F[s][g, r : r + SUB, :].astype(F32)
            v = jnp.concatenate([v[:, n : n + 128] * scale for n in range(0, nchan, 128)], 1)
            state = state * (decay[...] * keep[f + g]) + v
            pooled[window[f + g], rows, :] += state
        last[rows, :] = state

    products = [(m, n) for m in range(GROUP * TILE // ROWS) for n in range(0, nchan, 256)]

    def stage(later, ls, i, s):
        work = [(g, r) for r in range(0, TILE, SUB) for g in range(GROUP)] + [(None, r) for r in range(0, TILE, SUB)]
        todo = list(products)
        for at, (g, r) in enumerate(work):
            if todo and at * len(products) // len(work) >= len(products) - len(todo):
                product(later, ls, *todo.pop(0))
            if g is None:
                recur(i, s, r)
            else:
                activate(i, s, g, r)

    pieces = weights()
    for copy in pieces:
        copy.start()
    for q in range(tiles):
        prior(q).start()
        entering(q).start()
    last[...] = jnp.zeros_like(last)
    pooled[...] = jnp.zeros_like(pooled)
    for copy in pieces:
        copy.wait()
    prior(0).wait()
    entering(0).wait()
    for m, n in products:
        product(0, 0, m, n)

    def body(step, _):
        i = 2 * step

        @pl.when(step > 0)
        def _():
            leaving(i - 2, 0).wait()
            leaving(i - 1, 1).wait()

        stage(i + 1, 1, i, 0)
        leaving(i, 0).start()
        q = (i + 2) // groups

        @pl.when(jnp.logical_and(lax.rem(i + 2, groups) == 0, q < tiles))
        def _():
            prior(q).wait()
            entering(q).wait()

        stage(lax.rem(i + 2, total), 0, i + 1, 1)
        leaving(i + 1, 1).start()
        return 0

    lax.fori_loop(0, total // 2, body, 0)
    spread(high, low, scaled, last, pooled, sends, own)
    leaving(total - 2, 0).wait()
    leaving(total - 1, 1).wait()


def final_kernel(counts, *refs):
    per = counts.shape[0]
    latents = refs[-1]
    start = 0
    for index in range(len(refs) // 2):
        got, own = refs[2 * index], refs[2 * index + 1]
        ndev, rows, width = got.shape
        nproj = rows // per
        for i in range(per):
            part = slice(i * nproj, (i + 1) * nproj)
            total = own[part, :]
            for d in range(ndev):
                total = total + got[d, part, :].astype(F32)
            for n in range(0, width, 128):
                latents[i, :, start + n : start + n + 128] = total[:, n : n + 128] / counts[i : i + 1, :]
        start += width


def per_device(clips, w_time, gain, rate, keep, latent_ids, w_lat):
    _, nframe, npos, nchan = clips.shape
    nproj = w_lat.shape[1]
    ndev = lax.axis_size("tm")
    shards = lax.axis_size("dp")
    nall = nframe * ndev
    per = nframe // STRIDE
    nlat = per * ndev
    me = lax.axis_index("tm")
    side = me % 2
    x = clips[0]

    own_w = w_time * jnp.asarray(0.5, BF16)
    half = own_w.shape[1] // 2
    mine = lax.dynamic_slice_in_dim(own_w, side * half, half, 1)
    dc, da, db = rotated(mine, "dp", 2), rotated(mine, "dp", 1), rotated(mine, "dp", -1)
    sa, sb, sc = swapped(da, "tm"), swapped(db, "tm"), swapped(dc, "tm")
    source, keep, latent_ids, rate, gain, w_lat, _ = lax.optimization_barrier(
        (x, keep, latent_ids, rate, gain, w_lat, mine)
    )
    halo = shifted(source[nframe - (KT - 1) :], "tm", 1)
    lane = jnp.arange(128, dtype=jnp.int32)[None]
    local = jnp.where(lane < 64, keep[:, None], latent_ids.astype(F32)[:, None])
    local = jnp.broadcast_to(local[None], (ndev, nframe, 128))
    packed = lax.all_to_all(local, "tm", 0, 0).reshape(nall, 128)

    decay = jnp.exp(-rate)[None]
    inject = jnp.sqrt(-jnp.expm1(-2.0 * rate))
    scaled = w_lat.T.astype(F32) * (inject * gain)[None]

    vmem = pl.BlockSpec(memory_space=pltpu.VMEM)
    smem = pl.BlockSpec(memory_space=pltpu.SMEM)
    hbm = pl.BlockSpec(memory_space=pltpu.HBM)
    table_shape = jax.ShapeDtypeStruct((nlat, nproj, nchan), BF16)

    window = latent_ids - me.astype(jnp.int32) * per
    high, low, counts = pl.pallas_call(
        table_kernel,
        out_shape=(table_shape, table_shape, jax.ShapeDtypeStruct((per, 128), F32)),
        in_specs=[vmem] * 3,
        out_specs=(vmem,) * 3,
        scratch_shapes=[pltpu.VMEM((nall, nchan), F32)],
        compiler_params=pltpu.CompilerParams(vmem_limit_bytes=24 << 20),
        cost_estimate=pl.CostEstimate(
            flops=12 * nlat * nall * nchan, bytes_accessed=4 << 20, transcendentals=nall * nchan
        ),
        name="tables",
    )(packed, rate[None], scaled)
    stage_rows = GROUP * TILE
    features, sends, own = pl.pallas_call(
        functools.partial(conv_kernel, shards=shards),
        out_shape=(
            jax.ShapeDtypeStruct((nframe, npos, nchan), BF16),
            jax.ShapeDtypeStruct((ndev, per * nproj, npos), BF16),
            jax.ShapeDtypeStruct((per * nproj, npos), F32),
        ),
        in_specs=[smem, smem] + [hbm] * 9 + [vmem] * 4,
        out_specs=(hbm, vmem, vmem),
        scratch_shapes=[
            pltpu.VMEM((KT, nchan, nchan), BF16),
            pltpu.VMEM((nframe + KT - 1, npos, nchan), BF16),
            pltpu.VMEM((stage_rows, nchan), F32),
            pltpu.VMEM((stage_rows, nchan), F32),
            pltpu.VMEM((GROUP, TILE, nchan), BF16),
            pltpu.VMEM((GROUP, TILE, nchan), BF16),
            pltpu.VMEM((stage_rows, 128), F32),
            pltpu.VMEM((npos, nchan), F32),
            pltpu.VMEM((3, npos, nchan), F32),
            pltpu.SemaphoreType.DMA((7,)),
            pltpu.SemaphoreType.DMA((2 * npos // TILE,)),
            pltpu.SemaphoreType.DMA((2,)),
        ],
        compiler_params=pltpu.CompilerParams(vmem_limit_bytes=44 << 20),
        cost_estimate=pl.CostEstimate(
            flops=2 * KT * nframe * npos * nchan * nchan,
            bytes_accessed=4 * nframe * npos * nchan,
            transcendentals=nframe * npos * nchan,
        ),
        name="conv",
    )(window, keep, x, halo, own_w, da, db, dc, sa, sb, sc, decay, high, low, scaled)
    outs = [lax.all_to_all(sends, "tm", 0, 0), own]
    latents = pl.pallas_call(
        final_kernel,
        out_shape=jax.ShapeDtypeStruct((per, nproj, npos), F32),
        in_specs=[vmem] * (1 + len(outs)),
        out_specs=vmem,
        compiler_params=pltpu.CompilerParams(vmem_limit_bytes=16 << 20),
        name="final",
    )(counts, *outs)
    return features[None], latents[None]


def solution(mesh):
    return jax.shard_map(
        per_device,
        mesh=mesh,
        in_specs=(P("dp", "tm", None, None), P(None, "dp", None), P(), P(), P("tm"), P("tm"), P()),
        out_specs=(P("dp", "tm", None, None), P("dp", "tm", None, None)),
        check_vma=False,
    )
```

```python
import functools

import jax
import jax.numpy as jnp
from jax import lax
from jax.experimental import pallas as pl
from jax.experimental.pallas import tpu as pltpu
from jax.sharding import PartitionSpec as P


KT = 3
STRIDE = 8
F32 = jnp.float32
BF16 = jnp.bfloat16
TILE = 128
GROUP = 4
ROWS = 256
SUB = 16


def rotated(value, axis, steps):
    count = lax.axis_size(axis)
    return lax.ppermute(value, axis, [(s, (s + steps) % count) for s in range(count)])


def shifted(value, axis, steps):
    count = lax.axis_size(axis)
    return lax.ppermute(value, axis, [(s, s + steps) for s in range(count - steps)])


def swapped(value, axis):
    return lax.ppermute(value, axis, [(s, s ^ 1) for s in range(lax.axis_size(axis))])


def pack_kernel(keep, ids, out):
    ndev, nframe, lanes = out.shape
    row = lax.broadcasted_iota(jnp.int32, (nframe, lanes), 0)
    lane = lax.broadcasted_iota(jnp.int32, (nframe, lanes), 1)
    block = jnp.zeros((nframe, lanes), F32)
    for f in range(nframe):
        value = jnp.where(lane < lanes // 2, keep[f], ids[f].astype(F32))
        block = jnp.where(row == f, value, block)
    for d in range(ndev):
        out[d] = block


def table_kernel(packed, rate, scaled, high, low, counts, E):
    nall, lanes = packed.shape
    nchan = rate.shape[1]
    nlat = high.shape[0]
    me = lax.axis_index("tm")
    end = (me + 1) * (nall // lax.axis_size("tm")) - 1
    frame = lax.broadcasted_iota(jnp.int32, (nall, lanes), 0)
    logs = jnp.where(frame > end, jnp.log(jnp.maximum(packed[...], 0.5)), 0.0)
    rows = lax.broadcasted_iota(jnp.int32, (nall, nall), 0)
    cols = lax.broadcasted_iota(jnp.int32, (nall, nall), 1)
    run = jnp.dot(
        (cols <= rows).astype(F32), logs, precision=lax.Precision.HIGHEST, preferred_element_type=F32
    )
    block = 128
    for r in range(0, nall, block):
        at = lax.broadcasted_iota(jnp.int32, (block, nchan), 0) + r
        gap = (at - end).astype(F32)
        E[r : r + block, :] = jnp.where(at > end, jnp.exp(run[r : r + block, 0:1] - rate[...] * gap), 0.0)
    ids = packed[:, lanes // 2 : lanes // 2 + 1].astype(jnp.int32)
    member = (lax.broadcasted_iota(jnp.int32, (nall, lanes), 1) == ids).astype(F32)
    table = lax.dot_general(
        member, E[...], (((0,), (0,)), ((), ())), precision=lax.Precision.HIGHEST, preferred_element_type=F32
    )
    per = counts.shape[0]
    for i in range(per):
        hit = (jnp.broadcast_to(ids, (nall, lanes)) == me * per + i).astype(F32)
        counts[i : i + 1, :] = jnp.sum(hit, 0, keepdims=True)
    E[0:lanes, :] = table
    for j in range(nlat):
        value = scaled[...] * E[j : j + 1, :]
        upper = value.astype(BF16)
        high[j] = upper
        low[j] = (value - upper.astype(F32)).astype(BF16)


def times(a, b):
    return lax.dot_general(a, b, (((1,), (1,)), ((), ())), preferred_element_type=F32)


def split(value):
    upper = value.astype(BF16)
    return upper, (value - upper.astype(F32)).astype(BF16)


def spread_kernel(high, low, scaled, last, pooled, sends, own):
    nlat, nproj, nchan = high.shape
    ndev = sends.shape[0]
    width = last.shape[0]
    top, rest = split(last[...])
    rows = 256
    per = sends.shape[1]
    for r in range(0, nlat * nproj, rows):
        upper = high[r // nproj : (r + rows) // nproj].reshape(rows, nchan)
        lower = low[r // nproj : (r + rows) // nproj].reshape(rows, nchan)
        z = times(upper, top) + times(upper, rest) + times(lower, top)
        sends[r // per : (r + rows) // per] = z.reshape(rows // per, per, width).astype(BF16)
    upper, lower = split(scaled[...])
    parts = []
    for j in range(3):
        top, rest = split(pooled[j])
        parts.append(times(upper, top) + times(upper, rest) + times(lower, top))
    own[0:nproj, :] = parts[0]
    own[nproj : 2 * nproj, :] = parts[1]
    me = lax.axis_index("tm")

    @pl.when(me < ndev - 1)
    def _():
        block = sends[me + 1]
        sends[me + 1, 0:nproj] = (block[0:nproj].astype(F32) + parts[2]).astype(BF16)


def conv_kernel(
    ids, keep, x_hbm, halo_hbm, own_w, da, db, dc, sa, sb, sc, decay,
    feat_hbm, last, pooled, w, X, HA, HB, FA, FB, R, wsem, insem, outsem, *, shards,
):
    nframe, npos, nchan = x_hbm.shape
    tiles, groups = npos // TILE, nframe // GROUP
    total = tiles * groups
    H, F = (HA, HB), (FA, FB)
    half, depth = da.shape[1], own_w.shape[1]
    me = lax.axis_index("dp")
    side = lax.rem(lax.axis_index("tm"), 2)
    lead = KT - 1
    base = lax.axis_index("tm") * (nframe // STRIDE)

    def weights():
        copies = [pltpu.make_async_copy(own_w, w.at[:, pl.ds(pl.multiple_of(me * depth, depth), depth)], wsem.at[0])]
        slot = 1
        for step, mine, other in ((shards - 1, da, sa), (1, db, sb), (2, dc, sc)):
            base = lax.rem(me + step, shards) * depth
            for piece, lane in ((mine, side), (other, 1 - side)):
                row = pl.multiple_of(base + lane * half, half)
                copies.append(pltpu.make_async_copy(piece, w.at[:, pl.ds(row, half)], wsem.at[slot]))
                slot += 1
        return copies

    def entering(q):
        part = pl.ds(q * TILE, TILE)
        return pltpu.make_async_copy(x_hbm.at[:, part], X.at[lead : lead + nframe, part], insem.at[q])

    def prior(q):
        part = pl.ds(q * TILE, TILE)
        return pltpu.make_async_copy(halo_hbm.at[:, part], X.at[0:lead, part], insem.at[tiles + q])

    def place(i):
        return pl.multiple_of(i // groups * TILE, TILE), lax.rem(i, groups) * GROUP

    def leaving(i, s):
        p, f = place(i)
        return pltpu.make_async_copy(F[s], feat_hbm.at[pl.ds(f, GROUP), pl.ds(p, TILE)], outsem.at[s])

    def product(i, s, m, n):
        p, f = place(i)
        count = ROWS // TILE
        acc = None
        for k in range(KT):
            rows = X[pl.ds(f + lead - k + m * count, count), pl.ds(p, TILE), :].reshape(ROWS, nchan)
            part = jnp.dot(rows, w[k, :, n : n + 256], preferred_element_type=F32)
            acc = part if acc is None else acc + part
        H[s][m * ROWS : (m + 1) * ROWS, n : n + 256] = acc

    def activate(i, s, g, r):
        p, f = place(i)
        at = g * TILE + r
        h = H[s][at : at + SUB, :]
        c = X[f + lead + g, pl.ds(p + r, SUB), :].astype(F32)
        value = c + (h + h * jnp.tanh(h))
        F[s][g, r : r + SUB, :] = value.astype(BF16)
        mean = jnp.sum(value * value, -1, keepdims=True) * (1.0 / nchan)
        R[at : at + SUB, :] = jnp.broadcast_to(lax.rsqrt(mean + 1e-06), (SUB, 128))

    def recur(i, s, r):
        p, f = place(i)
        rows = pl.ds(p + r, SUB)
        state = last[rows, :]
        for g in range(GROUP):
            scale = R[g * TILE + r : g * TILE + r + SUB, :]
            v = F[s][g, r : r + SUB, :].astype(F32)
            v = jnp.concatenate([v[:, n : n + 128] * scale for n in range(0, nchan, 128)], 1)
            state = state * (decay[...] * keep[f + g]) + v
            pooled[ids[f + g] - base, rows, :] += state
        last[rows, :] = state

    products = [(m, n) for m in range(GROUP * TILE // ROWS) for n in range(0, nchan, 256)]

    def stage(later, ls, i, s):
        work = [(g, r) for r in range(0, TILE, SUB) for g in range(GROUP)] + [(None, r) for r in range(0, TILE, SUB)]
        todo = list(products)
        for at, (g, r) in enumerate(work):
            if todo and at * len(products) // len(work) >= len(products) - len(todo):
                product(later, ls, *todo.pop(0))
            if g is None:
                recur(i, s, r)
            else:
                activate(i, s, g, r)

    pieces = weights()
    for copy in pieces:
        copy.start()
    for q in range(tiles):
        prior(q).start()
        entering(q).start()
    last[...] = jnp.zeros_like(last)
    pooled[...] = jnp.zeros_like(pooled)
    for copy in pieces:
        copy.wait()
    prior(0).wait()
    entering(0).wait()
    for m, n in products:
        product(0, 0, m, n)

    def body(step, _):
        i = 2 * step

        @pl.when(step > 0)
        def _():
            leaving(i - 2, 0).wait()
            leaving(i - 1, 1).wait()

        stage(i + 1, 1, i, 0)
        leaving(i, 0).start()
        q = (i + 2) // groups

        @pl.when(jnp.logical_and(lax.rem(i + 2, groups) == 0, q < tiles))
        def _():
            prior(q).wait()
            entering(q).wait()

        stage(lax.rem(i + 2, total), 0, i + 1, 1)
        leaving(i + 1, 1).start()
        return 0

    lax.fori_loop(0, total // 2, body, 0)
    leaving(total - 2, 0).wait()
    leaving(total - 1, 1).wait()


def final_kernel(counts, *refs):
    per = counts.shape[0]
    latents = refs[-1]
    start = 0
    for index in range(len(refs) // 2):
        got, own = refs[2 * index], refs[2 * index + 1]
        ndev, rows, width = got.shape
        nproj = rows // per
        for i in range(per):
            part = slice(i * nproj, (i + 1) * nproj)
            total = own[part, :]
            for d in range(ndev):
                total = total + got[d, part, :].astype(F32)
            for n in range(0, width, 128):
                latents[i, :, start + n : start + n + 128] = total[:, n : n + 128] / counts[i : i + 1, :]
        start += width


def per_device(clips, w_time, gain, rate, keep, latent_ids, w_lat):
    _, nframe, npos, nchan = clips.shape
    nproj = w_lat.shape[1]
    ndev = lax.axis_size("tm")
    shards = lax.axis_size("dp")
    nall = nframe * ndev
    per = nframe // STRIDE
    nlat = per * ndev
    me = lax.axis_index("tm")
    side = me % 2
    x = clips[0]

    own_w = w_time * jnp.asarray(0.5, BF16)
    half = own_w.shape[1] // 2
    mine = lax.dynamic_slice_in_dim(own_w, side * half, half, 1)
    dc = rotated(mine, "dp", 2)
    da = rotated(mine, "dp", 1)
    db = rotated(mine, "dp", -1)
    sa, sb, sc = swapped(da, "tm"), swapped(db, "tm"), swapped(dc, "tm")
    source, rate, gain, w_lat, _ = lax.optimization_barrier((x, rate, gain, w_lat, mine))
    halo = shifted(source[nframe - (KT - 1) :], "tm", 1)
    local = pl.pallas_call(
        pack_kernel,
        out_shape=jax.ShapeDtypeStruct((ndev, nframe, 128), F32),
        in_specs=[pl.BlockSpec(memory_space=pltpu.SMEM)] * 2,
        out_specs=pl.BlockSpec(memory_space=pltpu.VMEM),
        compiler_params=pltpu.CompilerParams(vmem_limit_bytes=8 << 20),
        name="pack",
    )(keep, latent_ids)
    packed = lax.all_to_all(local, "tm", 0, 0).reshape(nall, 128)

    decay = jnp.exp(-rate)[None]
    inject = jnp.sqrt(-jnp.expm1(-2.0 * rate))
    scaled = w_lat.T.astype(F32) * (inject * gain)[None]

    vmem = pl.BlockSpec(memory_space=pltpu.VMEM)
    smem = pl.BlockSpec(memory_space=pltpu.SMEM)
    hbm = pl.BlockSpec(memory_space=pltpu.HBM)
    table_shape = jax.ShapeDtypeStruct((nlat, nproj, nchan), BF16)

    stage_rows = GROUP * TILE
    conv = pl.pallas_call(
        functools.partial(conv_kernel, shards=shards),
        out_shape=(
            jax.ShapeDtypeStruct((nframe, npos, nchan), BF16),
            jax.ShapeDtypeStruct((npos, nchan), F32),
            jax.ShapeDtypeStruct((3, npos, nchan), F32),
        ),
        in_specs=[smem, smem] + [hbm] * 9 + [vmem],
        out_specs=(hbm, vmem, vmem),
        scratch_shapes=[
            pltpu.VMEM((KT, nchan, nchan), BF16),
            pltpu.VMEM((nframe + KT - 1, npos, nchan), BF16),
            pltpu.VMEM((stage_rows, nchan), F32),
            pltpu.VMEM((stage_rows, nchan), F32),
            pltpu.VMEM((GROUP, TILE, nchan), BF16),
            pltpu.VMEM((GROUP, TILE, nchan), BF16),
            pltpu.VMEM((stage_rows, 128), F32),
            pltpu.SemaphoreType.DMA((7,)),
            pltpu.SemaphoreType.DMA((2 * npos // TILE,)),
            pltpu.SemaphoreType.DMA((2,)),
        ],
        compiler_params=pltpu.CompilerParams(vmem_limit_bytes=48 << 20),
        cost_estimate=pl.CostEstimate(
            flops=2 * KT * nframe * npos * nchan * nchan,
            bytes_accessed=4 * nframe * npos * nchan,
            transcendentals=nframe * npos * nchan,
        ),
        name="conv",
    )
    features, last, pooled = conv(latent_ids, keep, x, halo, own_w, da, db, dc, sa, sb, sc, decay)
    packed, last = lax.optimization_barrier((packed, last))
    high, low, counts = pl.pallas_call(
        table_kernel,
        out_shape=(table_shape, table_shape, jax.ShapeDtypeStruct((per, 128), F32)),
        in_specs=[vmem] * 3,
        out_specs=(vmem,) * 3,
        scratch_shapes=[pltpu.VMEM((nall, nchan), F32)],
        compiler_params=pltpu.CompilerParams(vmem_limit_bytes=16 << 20),
        cost_estimate=pl.CostEstimate(
            flops=12 * nlat * nall * nchan, bytes_accessed=4 << 20, transcendentals=nall * nchan
        ),
        name="tables",
    )(packed, rate[None], scaled)
    sends, own = pl.pallas_call(
        spread_kernel,
        out_shape=(
            jax.ShapeDtypeStruct((ndev, per * nproj, npos), BF16),
            jax.ShapeDtypeStruct((per * nproj, npos), F32),
        ),
        in_specs=[vmem] * 5,
        out_specs=(vmem, vmem),
        compiler_params=pltpu.CompilerParams(vmem_limit_bytes=24 << 20),
        name="spread",
    )(high, low, scaled, last, pooled)
    outs = [lax.all_to_all(sends, "tm", 0, 0), own]
    latents = pl.pallas_call(
        final_kernel,
        out_shape=jax.ShapeDtypeStruct((per, nproj, npos), F32),
        in_specs=[vmem] * (1 + len(outs)),
        out_specs=vmem,
        compiler_params=pltpu.CompilerParams(vmem_limit_bytes=16 << 20),
        name="final",
    )(counts, *outs)
    return features[None], latents[None]


def solution(mesh):
    return jax.shard_map(
        per_device,
        mesh=mesh,
        in_specs=(P("dp", "tm", None, None), P(None, "dp", None), P(), P(), P("tm"), P("tm"), P()),
        out_specs=(P("dp", "tm", None, None), P("dp", "tm", None, None)),
        check_vma=False,
    )
```

```python
import functools

import jax
import jax.numpy as jnp
from jax import lax
from jax.experimental import pallas as pl
from jax.experimental.pallas import tpu as pltpu
from jax.sharding import PartitionSpec as P


KT = 3
STRIDE = 8
F32 = jnp.float32
BF16 = jnp.bfloat16
TILE = 128
GROUP = 4
ROWS = 256
SUB = 16


def rotated(value, axis, steps):
    count = lax.axis_size(axis)
    return lax.ppermute(value, axis, [(s, (s + steps) % count) for s in range(count)])


def shifted(value, axis, steps):
    count = lax.axis_size(axis)
    return lax.ppermute(value, axis, [(s, s + steps) for s in range(count - steps)])


def swapped(value, axis):
    return lax.ppermute(value, axis, [(s, s ^ 1) for s in range(lax.axis_size(axis))])


def pieces_of(value):
    one = value.astype(BF16).astype(F32)
    two = (value - one).astype(BF16).astype(F32)
    return one, two, value - one - two


def table_kernel(packed, rate, scaled, high, low, counts, E):
    nall, lanes = packed.shape
    nchan = rate.shape[1]
    nlat = high.shape[0]
    me = lax.axis_index("tm")
    end = (me + 1) * (nall // lax.axis_size("tm")) - 1
    frame = lax.broadcasted_iota(jnp.int32, (nall, lanes), 0)
    lane = lax.broadcasted_iota(jnp.int32, (nall, lanes), 1)
    logs = jnp.where(frame > end, jnp.log(packed[:, 0:1]), 0.0)
    one, two, three = pieces_of(logs)
    pieces = jnp.where(lane == 0, one, jnp.where(lane == 1, two, jnp.where(lane == 2, three, 0.0)))
    rows = lax.broadcasted_iota(jnp.int32, (nall, nall), 0)
    cols = lax.broadcasted_iota(jnp.int32, (nall, nall), 1)
    lower = jnp.where(cols <= rows, 1.0, 0.0).astype(BF16)
    run = jnp.dot(lower, pieces.astype(BF16), preferred_element_type=F32)
    run = jnp.sum(run, -1, keepdims=True)
    block = 128
    for r in range(0, nall, block):
        at = lax.broadcasted_iota(jnp.int32, (block, nchan), 0) + r
        gap = (at - end).astype(F32)
        E[r : r + block, :] = jnp.where(at > end, jnp.exp(run[r : r + block] - rate[...] * gap), 0.0)
    ids = packed[:, lanes // 2 : lanes // 2 + 1].astype(jnp.int32)
    member = jnp.where(lane == ids, 1.0, 0.0).astype(BF16)
    table = jnp.zeros((lanes, nchan), F32)
    for piece in pieces_of(E[...]):
        table = table + lax.dot_general(
            member, piece.astype(BF16), (((0,), (0,)), ((), ())), preferred_element_type=F32
        )
    per = counts.shape[0]
    for i in range(per):
        hit = (jnp.broadcast_to(ids, (nall, lanes)) == me * per + i).astype(F32)
        counts[i : i + 1, :] = jnp.sum(hit, 0, keepdims=True)
    E[0:lanes, :] = table
    for j in range(nlat):
        value = scaled[...] * E[j : j + 1, :]
        upper = value.astype(BF16)
        high[j] = upper
        low[j] = (value - upper.astype(F32)).astype(BF16)


def times(a, b):
    return lax.dot_general(a, b, (((1,), (1,)), ((), ())), preferred_element_type=F32)


def split(value):
    upper = value.astype(BF16)
    return upper, (value - upper.astype(F32)).astype(BF16)


def spread_kernel(high, low, last, own, sends):
    nlat, nproj, nchan = high.shape
    ndev, per, width = sends.shape
    top, rest = split(last[...])
    rows = 256
    for r in range(0, nlat * nproj, rows):
        upper = high[r // nproj : (r + rows) // nproj].reshape(rows, nchan)
        lower = low[r // nproj : (r + rows) // nproj].reshape(rows, nchan)
        z = times(upper, top) + times(upper, rest) + times(lower, top)
        sends[r // per : (r + rows) // per] = z.reshape(rows // per, per, width).astype(BF16)
    me = lax.axis_index("tm")

    @pl.when(me < ndev - 1)
    def _():
        block = sends[me + 1]
        moved = own[2 * nproj : 3 * nproj, :]
        sends[me + 1, 0:nproj] = (block[0:nproj].astype(F32) + moved).astype(BF16)


def conv_kernel(
    window, keep, x_hbm, halo_hbm, own_w, da, db, dc, sa, sb, sc, decay, scaled,
    feat_hbm, last, sums, w, X, HA, HB, FA, FB, R, pooled, wsem, insem, outsem, *, shards,
):
    nframe, npos, nchan = x_hbm.shape
    tiles, groups = npos // TILE, nframe // GROUP
    total = tiles * groups
    H, F = (HA, HB), (FA, FB)
    half, depth = da.shape[1], own_w.shape[1]
    me = lax.axis_index("dp")
    side = lax.rem(lax.axis_index("tm"), 2)
    lead = KT - 1

    def weights():
        copies = [pltpu.make_async_copy(own_w, w.at[:, pl.ds(pl.multiple_of(me * depth, depth), depth)], wsem.at[0])]
        slot = 1
        for step, mine, other in ((shards - 1, da, sa), (1, db, sb), (2, dc, sc)):
            base = lax.rem(me + step, shards) * depth
            for piece, lane in ((mine, side), (other, 1 - side)):
                row = pl.multiple_of(base + lane * half, half)
                copies.append(pltpu.make_async_copy(piece, w.at[:, pl.ds(row, half)], wsem.at[slot]))
                slot += 1
        return copies

    def entering(q):
        part = pl.ds(q * TILE, TILE)
        return pltpu.make_async_copy(x_hbm.at[:, part], X.at[lead : lead + nframe, part], insem.at[q])

    def prior(q):
        part = pl.ds(q * TILE, TILE)
        return pltpu.make_async_copy(halo_hbm.at[:, part], X.at[0:lead, part], insem.at[tiles + q])

    def place(i):
        return pl.multiple_of(i // groups * TILE, TILE), lax.rem(i, groups) * GROUP

    def leaving(i, s):
        p, f = place(i)
        return pltpu.make_async_copy(F[s], feat_hbm.at[pl.ds(f, GROUP), pl.ds(p, TILE)], outsem.at[s])

    def product(i, s, m, n):
        p, f = place(i)
        count = ROWS // TILE
        acc = None
        for k in range(KT):
            rows = X[pl.ds(f + lead - k + m * count, count), pl.ds(p, TILE), :].reshape(ROWS, nchan)
            part = jnp.dot(rows, w[k, :, n : n + 256], preferred_element_type=F32)
            acc = part if acc is None else acc + part
        H[s][m * ROWS : (m + 1) * ROWS, n : n + 256] = acc

    def activate(i, s, g, r):
        p, f = place(i)
        at = g * TILE + r
        h = H[s][at : at + SUB, :]
        c = X[f + lead + g, pl.ds(p + r, SUB), :].astype(F32)
        value = c + (h + h * jnp.tanh(h))
        F[s][g, r : r + SUB, :] = value.astype(BF16)
        mean = jnp.sum(value * value, -1, keepdims=True) * (1.0 / nchan)
        R[at : at + SUB, :] = jnp.broadcast_to(lax.rsqrt(mean + 1e-06), (SUB, 128))

    def recur(i, s, r):
        p, f = place(i)
        rows = pl.ds(p + r, SUB)
        state = last[rows, :]
        for g in range(GROUP):
            scale = R[g * TILE + r : g * TILE + r + SUB, :]
            v = F[s][g, r : r + SUB, :].astype(F32)
            v = jnp.concatenate([v[:, n : n + 128] * scale for n in range(0, nchan, 128)], 1)
            state = state * (decay[...] * keep[f + g]) + v
            pooled[window[f + g], rows, :] += state
        last[rows, :] = state

    products = [(m, n) for m in range(GROUP * TILE // ROWS) for n in range(0, nchan, 256)]

    def stage(later, ls, i, s):
        work = [(g, r) for r in range(0, TILE, SUB) for g in range(GROUP)] + [(None, r) for r in range(0, TILE, SUB)]
        todo = list(products)
        for at, (g, r) in enumerate(work):
            if todo and at * len(products) // len(work) >= len(products) - len(todo):
                product(later, ls, *todo.pop(0))
            if g is None:
                recur(i, s, r)
            else:
                activate(i, s, g, r)

    pieces = weights()
    for copy in pieces:
        copy.start()
    for q in range(tiles):
        prior(q).start()
        entering(q).start()
    last[...] = jnp.zeros_like(last)
    pooled[...] = jnp.zeros_like(pooled)
    for copy in pieces:
        copy.wait()
    prior(0).wait()
    entering(0).wait()
    for m, n in products:
        product(0, 0, m, n)

    def body(step, _):
        i = 2 * step

        @pl.when(step > 0)
        def _():
            leaving(i - 2, 0).wait()
            leaving(i - 1, 1).wait()

        stage(i + 1, 1, i, 0)
        leaving(i, 0).start()
        q = (i + 2) // groups

        @pl.when(jnp.logical_and(lax.rem(i + 2, groups) == 0, q < tiles))
        def _():
            prior(q).wait()
            entering(q).wait()

        stage(lax.rem(i + 2, total), 0, i + 1, 1)
        leaving(i + 1, 1).start()
        return 0

    lax.fori_loop(0, total // 2, body, 0)
    nproj = scaled.shape[0]
    upper, lower = split(scaled[...])
    both = jnp.concatenate([upper, lower], 0)
    for j in range(3):
        top, rest = split(pooled[j])
        part = times(both, top)
        sums[j * nproj : (j + 1) * nproj, :] = part[:nproj] + part[nproj:] + times(upper, rest)
    leaving(total - 2, 0).wait()
    leaving(total - 1, 1).wait()


def final_kernel(counts, *refs):
    per = counts.shape[0]
    latents = refs[-1]
    start = 0
    for index in range(len(refs) // 2):
        got, own = refs[2 * index], refs[2 * index + 1]
        ndev, rows, width = got.shape
        nproj = rows // per
        for i in range(per):
            part = slice(i * nproj, (i + 1) * nproj)
            total = own[part, :]
            for d in range(ndev):
                total = total + got[d, part, :].astype(F32)
            for n in range(0, width, 128):
                latents[i, :, start + n : start + n + 128] = total[:, n : n + 128] / counts[i : i + 1, :]
        start += width


def per_device(clips, w_time, gain, rate, keep, latent_ids, w_lat):
    _, nframe, npos, nchan = clips.shape
    nproj = w_lat.shape[1]
    ndev = lax.axis_size("tm")
    shards = lax.axis_size("dp")
    nall = nframe * ndev
    per = nframe // STRIDE
    nlat = per * ndev
    me = lax.axis_index("tm")
    side = me % 2
    x = clips[0]

    own_w = w_time * jnp.asarray(0.5, BF16)
    half = own_w.shape[1] // 2
    mine = lax.dynamic_slice_in_dim(own_w, side * half, half, 1)
    dc = rotated(mine, "dp", 2)
    da = rotated(mine, "dp", 1)
    db = rotated(mine, "dp", -1)
    sa, sb, sc = swapped(da, "tm"), swapped(db, "tm"), swapped(dc, "tm")
    rate, gain, w_lat, _ = lax.optimization_barrier((rate, gain, w_lat, mine))
    halo = shifted(x[nframe - (KT - 1) :], "tm", 1)
    window = latent_ids - me.astype(jnp.int32) * per
    keep = jnp.where(latent_ids < 0, 0.0, keep)
    lane = jnp.arange(128, dtype=jnp.int32)[None]
    local = jnp.where(lane < 64, keep[:, None], latent_ids.astype(F32)[:, None])
    local = jnp.broadcast_to(local[None], (ndev, nframe, 128))
    packed = lax.all_to_all(local, "tm", 0, 0).reshape(nall, 128)

    decay = jnp.exp(-rate)[None]
    inject = jnp.sqrt(-jnp.expm1(-2.0 * rate))
    scaled = w_lat.T.astype(F32) * (inject * gain)[None]

    vmem = pl.BlockSpec(memory_space=pltpu.VMEM)
    smem = pl.BlockSpec(memory_space=pltpu.SMEM)
    hbm = pl.BlockSpec(memory_space=pltpu.HBM)
    table_shape = jax.ShapeDtypeStruct((nlat, nproj, nchan), BF16)

    stage_rows = GROUP * TILE
    conv = pl.pallas_call(
        functools.partial(conv_kernel, shards=shards),
        out_shape=(
            jax.ShapeDtypeStruct((nframe, npos, nchan), BF16),
            jax.ShapeDtypeStruct((npos, nchan), F32),
            jax.ShapeDtypeStruct((3 * nproj, npos), F32),
        ),
        in_specs=[smem, smem] + [hbm] * 9 + [vmem] * 2,
        out_specs=(hbm, vmem, vmem),
        scratch_shapes=[
            pltpu.VMEM((KT, nchan, nchan), BF16),
            pltpu.VMEM((nframe + KT - 1, npos, nchan), BF16),
            pltpu.VMEM((stage_rows, nchan), F32),
            pltpu.VMEM((stage_rows, nchan), F32),
            pltpu.VMEM((GROUP, TILE, nchan), BF16),
            pltpu.VMEM((GROUP, TILE, nchan), BF16),
            pltpu.VMEM((stage_rows, 128), F32),
            pltpu.VMEM((3, npos, nchan), F32),
            pltpu.SemaphoreType.DMA((7,)),
            pltpu.SemaphoreType.DMA((2 * npos // TILE,)),
            pltpu.SemaphoreType.DMA((2,)),
        ],
        compiler_params=pltpu.CompilerParams(vmem_limit_bytes=48 << 20),
        cost_estimate=pl.CostEstimate(
            flops=2 * KT * nframe * npos * nchan * nchan,
            bytes_accessed=4 * nframe * npos * nchan,
            transcendentals=nframe * npos * nchan,
        ),
        name="conv",
    )
    features, last, own = conv(window, keep, x, halo, own_w, da, db, dc, sa, sb, sc, decay, scaled)
    packed, last = lax.optimization_barrier((packed, last))
    high, low, counts = pl.pallas_call(
        table_kernel,
        out_shape=(table_shape, table_shape, jax.ShapeDtypeStruct((per, 128), F32)),
        in_specs=[vmem] * 3,
        out_specs=(vmem,) * 3,
        scratch_shapes=[pltpu.VMEM((nall, nchan), F32)],
        compiler_params=pltpu.CompilerParams(vmem_limit_bytes=16 << 20),
        cost_estimate=pl.CostEstimate(
            flops=12 * nlat * nall * nchan, bytes_accessed=4 << 20, transcendentals=nall * nchan
        ),
        name="tables",
    )(packed, rate[None], scaled)
    sends = pl.pallas_call(
        spread_kernel,
        out_shape=jax.ShapeDtypeStruct((ndev, per * nproj, npos), BF16),
        in_specs=[vmem] * 4,
        out_specs=vmem,
        compiler_params=pltpu.CompilerParams(vmem_limit_bytes=16 << 20),
        name="spread",
    )(high, low, last, own)
    outs = [lax.all_to_all(sends, "tm", 0, 0), own]
    latents = pl.pallas_call(
        final_kernel,
        out_shape=jax.ShapeDtypeStruct((per, nproj, npos), F32),
        in_specs=[vmem] * (1 + len(outs)),
        out_specs=vmem,
        compiler_params=pltpu.CompilerParams(vmem_limit_bytes=16 << 20),
        name="final",
    )(counts, *outs)
    return features[None], latents[None]


def solution(mesh):
    return jax.shard_map(
        per_device,
        mesh=mesh,
        in_specs=(P("dp", "tm", None, None), P(None, "dp", None), P(), P(), P("tm"), P("tm"), P()),
        out_specs=(P("dp", "tm", None, None), P("dp", "tm", None, None)),
        check_vma=False,
    )
```

```python
import functools

import jax
import jax.numpy as jnp
from jax import lax
from jax.experimental import pallas as pl
from jax.experimental.pallas import tpu as pltpu
from jax.sharding import PartitionSpec as P


KT = 3
STRIDE = 8
F32 = jnp.float32
BF16 = jnp.bfloat16
TILE = 128
GROUP = 4
ROWS = 256
SUB = 16


def rotated(value, axis, steps):
    count = lax.axis_size(axis)
    return lax.ppermute(value, axis, [(s, (s + steps) % count) for s in range(count)])


def shifted(value, axis, steps):
    count = lax.axis_size(axis)
    return lax.ppermute(value, axis, [(s, s + steps) for s in range(count - steps)])


def swapped(value, axis):
    return lax.ppermute(value, axis, [(s, s ^ 1) for s in range(lax.axis_size(axis))])


def pieces_of(value):
    one = value.astype(BF16).astype(F32)
    two = (value - one).astype(BF16).astype(F32)
    return one, two, value - one - two


def table_kernel(packed, rate, constants, high, low, counts, E):
    nall, lanes = packed.shape
    nchan = rate.shape[1]
    nlat = high.shape[0]
    me = lax.axis_index("tm")
    end = (me + 1) * (nall // lax.axis_size("tm")) - 1
    frame = lax.broadcasted_iota(jnp.int32, (nall, lanes), 0)
    lane = lax.broadcasted_iota(jnp.int32, (nall, lanes), 1)
    logs = jnp.where(frame > end, jnp.log(packed[:, 0:1]), 0.0)
    one, two, three = pieces_of(logs)
    pieces = jnp.where(lane == 0, one, jnp.where(lane == 1, two, jnp.where(lane == 2, three, 0.0)))
    rows = lax.broadcasted_iota(jnp.int32, (nall, nall), 0)
    cols = lax.broadcasted_iota(jnp.int32, (nall, nall), 1)
    lower = jnp.where(cols <= rows, 1.0, 0.0).astype(BF16)
    run = jnp.dot(lower, pieces.astype(BF16), preferred_element_type=F32)
    run = jnp.sum(run, -1, keepdims=True)
    block = 128
    for r in range(0, nall, block):
        at = lax.broadcasted_iota(jnp.int32, (block, nchan), 0) + r
        gap = (at - end).astype(F32)
        E[r : r + block, :] = jnp.where(at > end, jnp.exp(run[r : r + block] - rate[...] * gap), 0.0)
    ids = packed[:, lanes // 2 : lanes // 2 + 1].astype(jnp.int32)
    member = jnp.where(lane == ids, 1.0, 0.0).astype(BF16)
    table = jnp.zeros((lanes, nchan), F32)
    for piece in pieces_of(E[...]):
        table = table + lax.dot_general(
            member, piece.astype(BF16), (((0,), (0,)), ((), ())), preferred_element_type=F32
        )
    per = counts.shape[0]
    for i in range(per):
        hit = (jnp.broadcast_to(ids, (nall, lanes)) == me * per + i).astype(F32)
        counts[i : i + 1, :] = jnp.sum(hit, 0, keepdims=True)
    E[0:lanes, :] = table
    scaled = constants[0 : high.shape[1], :]
    for j in range(nlat):
        value = scaled * E[j : j + 1, :]
        upper = value.astype(BF16)
        high[j] = upper
        low[j] = (value - upper.astype(F32)).astype(BF16)


def times(a, b):
    return lax.dot_general(a, b, (((1,), (1,)), ((), ())), preferred_element_type=F32)


def split(value):
    upper = value.astype(BF16)
    return upper, (value - upper.astype(F32)).astype(BF16)


def spread_kernel(high, low, last, own, sends):
    nlat, nproj, nchan = high.shape
    ndev, per, width = sends.shape
    top, rest = split(last[...])
    rows = 256
    for r in range(0, nlat * nproj, rows):
        upper = high[r // nproj : (r + rows) // nproj].reshape(rows, nchan)
        lower = low[r // nproj : (r + rows) // nproj].reshape(rows, nchan)
        z = times(upper, top) + times(upper, rest) + times(lower, top)
        sends[r // per : (r + rows) // per] = z.reshape(rows // per, per, width).astype(BF16)
    me = lax.axis_index("tm")

    @pl.when(me < ndev - 1)
    def _():
        block = sends[me + 1]
        moved = own[2 * nproj : 3 * nproj, :]
        sends[me + 1, 0:nproj] = (block[0:nproj].astype(F32) + moved).astype(BF16)


def conv_kernel(
    window, packing, x_hbm, halo_hbm, mine, da, db, dc, so, sa, sb, sc, constants,
    feat_hbm, last, sums, w, X, HA, HB, FA, FB, R, pooled, kept, wsem, insem, outsem, *, shards,
):
    nframe, npos, nchan = x_hbm.shape
    tiles, groups = npos // TILE, nframe // GROUP
    total = tiles * groups
    H, F = (HA, HB), (FA, FB)
    half = da.shape[1]
    depth = 2 * half
    nproj = sums.shape[0] // 3
    me = lax.axis_index("dp")
    side = lax.rem(lax.axis_index("tm"), 2)
    lead = KT - 1

    def weights():
        copies = []
        slot = 0
        for step, near, far in ((0, mine, so), (shards - 1, da, sa), (1, db, sb), (2, dc, sc)):
            base = lax.rem(me + step, shards) * depth
            for piece, lane in ((near, side), (far, 1 - side)):
                row = pl.multiple_of(base + lane * half, half)
                copies.append(pltpu.make_async_copy(piece, w.at[:, pl.ds(row, half)], wsem.at[slot]))
                slot += 1
        return copies

    def entering(q):
        part = pl.ds(q * TILE, TILE)
        return pltpu.make_async_copy(x_hbm.at[:, part], X.at[lead : lead + nframe, part], insem.at[q])

    def prior(q):
        part = pl.ds(q * TILE, TILE)
        return pltpu.make_async_copy(halo_hbm.at[:, part], X.at[0:lead, part], insem.at[tiles + q])

    def place(i):
        return pl.multiple_of(i // groups * TILE, TILE), lax.rem(i, groups) * GROUP

    def leaving(i, s):
        p, f = place(i)
        return pltpu.make_async_copy(F[s], feat_hbm.at[pl.ds(f, GROUP), pl.ds(p, TILE)], outsem.at[s])

    def product(i, s, m, n):
        p, f = place(i)
        count = ROWS // TILE
        acc = None
        for k in range(KT):
            rows = X[pl.ds(f + lead - k + m * count, count), pl.ds(p, TILE), :].reshape(ROWS, nchan)
            part = jnp.dot(rows, w[k, :, n : n + 256], preferred_element_type=F32)
            acc = part if acc is None else acc + part
        H[s][m * ROWS : (m + 1) * ROWS, n : n + 256] = acc

    def activate(i, s, g, r):
        p, f = place(i)
        at = g * TILE + r
        h = H[s][at : at + SUB, :]
        c = X[f + lead + g, pl.ds(p + r, SUB), :].astype(F32)
        value = c + (h + h * jnp.tanh(h))
        F[s][g, r : r + SUB, :] = value.astype(BF16)
        mean = jnp.sum(value * value, -1, keepdims=True) * (1.0 / nchan)
        R[at : at + SUB, :] = jnp.broadcast_to(lax.rsqrt(mean + 1e-06), (SUB, 128))

    def recur(i, s, r):
        p, f = place(i)
        rows = pl.ds(p + r, SUB)
        state = last[rows, :]
        for g in range(GROUP):
            scale = R[g * TILE + r : g * TILE + r + SUB, :]
            v = F[s][g, r : r + SUB, :].astype(F32)
            v = jnp.concatenate([v[:, n : n + 128] * scale for n in range(0, nchan, 128)], 1)
            state = state * kept[pl.ds(f + g, 1), :] + v
            pooled[window[f + g], rows, :] += state
        last[rows, :] = state

    products = [(m, n) for m in range(GROUP * TILE // ROWS) for n in range(0, nchan, 256)]

    def stage(later, ls, i, s):
        work = [(g, r) for r in range(0, TILE, SUB) for g in range(GROUP)] + [(None, r) for r in range(0, TILE, SUB)]
        todo = list(products)
        for at, (g, r) in enumerate(work):
            if todo and at * len(products) // len(work) >= len(products) - len(todo):
                product(later, ls, *todo.pop(0))
            if g is None:
                recur(i, s, r)
            else:
                activate(i, s, g, r)

    pieces = weights()
    for copy in pieces:
        copy.start()
    for q in range(tiles):
        prior(q).start()
        entering(q).start()
    kept[...] = constants[nproj : nproj + 1, :] * packing[:, 0:1]
    last[...] = jnp.zeros_like(last)
    pooled[...] = jnp.zeros_like(pooled)
    for copy in pieces:
        copy.wait()
    prior(0).wait()
    entering(0).wait()
    for m, n in products:
        product(0, 0, m, n)

    def body(step, _):
        i = 2 * step

        @pl.when(step > 0)
        def _():
            leaving(i - 2, 0).wait()
            leaving(i - 1, 1).wait()

        stage(i + 1, 1, i, 0)
        leaving(i, 0).start()
        q = (i + 2) // groups

        @pl.when(jnp.logical_and(lax.rem(i + 2, groups) == 0, q < tiles))
        def _():
            prior(q).wait()
            entering(q).wait()

        stage(lax.rem(i + 2, total), 0, i + 1, 1)
        leaving(i + 1, 1).start()
        return 0

    lax.fori_loop(0, total // 2, body, 0)
    upper, lower = split(constants[0:nproj, :])
    both = jnp.concatenate([upper, lower], 0)
    for j in range(3):
        top, rest = split(pooled[j])
        part = times(both, top)
        sums[j * nproj : (j + 1) * nproj, :] = part[:nproj] + part[nproj:] + times(upper, rest)
    leaving(total - 2, 0).wait()
    leaving(total - 1, 1).wait()


def final_kernel(counts, *refs):
    per = counts.shape[0]
    latents = refs[-1]
    start = 0
    for index in range(len(refs) // 2):
        got, own = refs[2 * index], refs[2 * index + 1]
        ndev, rows, width = got.shape
        nproj = rows // per
        for i in range(per):
            part = slice(i * nproj, (i + 1) * nproj)
            total = own[part, :]
            for d in range(ndev):
                total = total + got[d, part, :].astype(F32)
            for n in range(0, width, 128):
                latents[i, :, start + n : start + n + 128] = total[:, n : n + 128] / counts[i : i + 1, :]
        start += width


def per_device(clips, w_time, gain, rate, keep, latent_ids, w_lat):
    _, nframe, npos, nchan = clips.shape
    nproj = w_lat.shape[1]
    ndev = lax.axis_size("tm")
    shards = lax.axis_size("dp")
    nall = nframe * ndev
    per = nframe // STRIDE
    nlat = per * ndev
    me = lax.axis_index("tm")
    side = me % 2
    x = clips[0]

    half = w_time.shape[1] // 2
    mine = lax.dynamic_slice_in_dim(w_time, side * half, half, 1) * jnp.asarray(0.5, BF16)
    dc = rotated(mine, "dp", 2)
    da = rotated(mine, "dp", 1)
    db = rotated(mine, "dp", -1)
    so = swapped(mine, "tm")
    sa, sb, sc = swapped(da, "tm"), swapped(db, "tm"), swapped(dc, "tm")
    rate, gain, w_lat, _ = lax.optimization_barrier((rate, gain, w_lat, mine))
    halo = shifted(x[nframe - (KT - 1) :], "tm", 1)
    window = latent_ids - me.astype(jnp.int32) * per
    lane = jnp.arange(128, dtype=jnp.int32)[None]
    packing = jnp.where(lane < 64, keep[:, None], latent_ids.astype(F32)[:, None])
    local = jnp.broadcast_to(packing[None], (ndev, nframe, 128))
    packed = lax.all_to_all(local, "tm", 0, 0).reshape(nall, 128)

    inject = jnp.sqrt(-jnp.expm1(-2.0 * rate))
    row = jnp.arange(nproj + 8, dtype=jnp.int32)[:, None]
    padded = jnp.pad(w_lat.T.astype(F32), ((0, 8), (0, 0)))
    constants = jnp.where(row < nproj, padded * (inject * gain)[None], jnp.exp(-rate)[None])

    vmem = pl.BlockSpec(memory_space=pltpu.VMEM)
    smem = pl.BlockSpec(memory_space=pltpu.SMEM)
    hbm = pl.BlockSpec(memory_space=pltpu.HBM)
    table_shape = jax.ShapeDtypeStruct((nlat, nproj, nchan), BF16)

    stage_rows = GROUP * TILE
    conv = pl.pallas_call(
        functools.partial(conv_kernel, shards=shards),
        out_shape=(
            jax.ShapeDtypeStruct((nframe, npos, nchan), BF16),
            jax.ShapeDtypeStruct((npos, nchan), F32),
            jax.ShapeDtypeStruct((3 * nproj, npos), F32),
        ),
        in_specs=[smem, vmem] + [hbm] * 10 + [vmem],
        out_specs=(hbm, vmem, vmem),
        scratch_shapes=[
            pltpu.VMEM((KT, nchan, nchan), BF16),
            pltpu.VMEM((nframe + KT - 1, npos, nchan), BF16),
            pltpu.VMEM((stage_rows, nchan), F32),
            pltpu.VMEM((stage_rows, nchan), F32),
            pltpu.VMEM((GROUP, TILE, nchan), BF16),
            pltpu.VMEM((GROUP, TILE, nchan), BF16),
            pltpu.VMEM((stage_rows, 128), F32),
            pltpu.VMEM((3, npos, nchan), F32),
            pltpu.VMEM((nframe, nchan), F32),
            pltpu.SemaphoreType.DMA((8,)),
            pltpu.SemaphoreType.DMA((2 * npos // TILE,)),
            pltpu.SemaphoreType.DMA((2,)),
        ],
        compiler_params=pltpu.CompilerParams(vmem_limit_bytes=48 << 20),
        cost_estimate=pl.CostEstimate(
            flops=2 * KT * nframe * npos * nchan * nchan,
            bytes_accessed=4 * nframe * npos * nchan,
            transcendentals=nframe * npos * nchan,
        ),
        name="conv",
    )
    features, last, own = conv(window, packing, x, halo, mine, da, db, dc, so, sa, sb, sc, constants)
    packed, last = lax.optimization_barrier((packed, last))
    high, low, counts = pl.pallas_call(
        table_kernel,
        out_shape=(table_shape, table_shape, jax.ShapeDtypeStruct((per, 128), F32)),
        in_specs=[vmem] * 3,
        out_specs=(vmem,) * 3,
        scratch_shapes=[pltpu.VMEM((nall, nchan), F32)],
        compiler_params=pltpu.CompilerParams(vmem_limit_bytes=16 << 20),
        cost_estimate=pl.CostEstimate(
            flops=12 * nlat * nall * nchan, bytes_accessed=4 << 20, transcendentals=nall * nchan
        ),
        name="tables",
    )(packed, rate[None], constants)
    sends = pl.pallas_call(
        spread_kernel,
        out_shape=jax.ShapeDtypeStruct((ndev, per * nproj, npos), BF16),
        in_specs=[vmem] * 4,
        out_specs=vmem,
        compiler_params=pltpu.CompilerParams(vmem_limit_bytes=16 << 20),
        name="spread",
    )(high, low, last, own)
    outs = [lax.all_to_all(sends, "tm", 0, 0), own]
    latents = pl.pallas_call(
        final_kernel,
        out_shape=jax.ShapeDtypeStruct((per, nproj, npos), F32),
        in_specs=[vmem] * (1 + len(outs)),
        out_specs=vmem,
        compiler_params=pltpu.CompilerParams(vmem_limit_bytes=16 << 20),
        name="final",
    )(counts, *outs)
    return features[None], latents[None]


def solution(mesh):
    return jax.shard_map(
        per_device,
        mesh=mesh,
        in_specs=(P("dp", "tm", None, None), P(None, "dp", None), P(), P(), P("tm"), P("tm"), P()),
        out_specs=(P("dp", "tm", None, None), P("dp", "tm", None, None)),
        check_vma=False,
    )
```

```python
import functools

import jax
import jax.numpy as jnp
from jax import lax
from jax.experimental import pallas as pl
from jax.experimental.pallas import tpu as pltpu
from jax.sharding import PartitionSpec as P


KT = 3
STRIDE = 8
F32 = jnp.float32
BF16 = jnp.bfloat16
TILE = 128
GROUP = 4
ROWS = 256
SUB = 16


def rotated(value, axis, steps):
    count = lax.axis_size(axis)
    return lax.ppermute(value, axis, [(s, (s + steps) % count) for s in range(count)])


def shifted(value, axis, steps):
    count = lax.axis_size(axis)
    return lax.ppermute(value, axis, [(s, s + steps) for s in range(count - steps)])


def swapped(value, axis):
    return lax.ppermute(value, axis, [(s, s ^ 1) for s in range(lax.axis_size(axis))])


def pieces_of(value):
    one = value.astype(BF16).astype(F32)
    two = (value - one).astype(BF16).astype(F32)
    return one, two, value - one - two


def table_kernel(packed, rate, constants, high, low, counts, E):
    nall, lanes = packed.shape
    nchan = rate.shape[1]
    nlat = high.shape[0]
    me = lax.axis_index("tm")
    end = (me + 1) * (nall // lax.axis_size("tm")) - 1
    frame = lax.broadcasted_iota(jnp.int32, (nall, lanes), 0)
    lane = lax.broadcasted_iota(jnp.int32, (nall, lanes), 1)
    logs = jnp.where(frame > end, jnp.log(packed[:, 0:1]), 0.0)
    one, two, three = pieces_of(logs)
    pieces = jnp.where(lane == 0, one, jnp.where(lane == 1, two, jnp.where(lane == 2, three, 0.0)))
    rows = lax.broadcasted_iota(jnp.int32, (nall, nall), 0)
    cols = lax.broadcasted_iota(jnp.int32, (nall, nall), 1)
    lower = jnp.where(cols <= rows, 1.0, 0.0).astype(BF16)
    run = jnp.dot(lower, pieces.astype(BF16), preferred_element_type=F32)
    run = jnp.sum(run, -1, keepdims=True)
    block = 128
    for r in range(0, nall, block):
        at = lax.broadcasted_iota(jnp.int32, (block, nchan), 0) + r
        gap = (at - end).astype(F32)
        E[r : r + block, :] = jnp.where(at > end, jnp.exp(run[r : r + block] - rate[...] * gap), 0.0)
    ids = packed[:, lanes // 2 : lanes // 2 + 1].astype(jnp.int32)
    member = jnp.where(lane == ids, 1.0, 0.0).astype(BF16)
    table = jnp.zeros((lanes, nchan), F32)
    for piece in pieces_of(E[...]):
        table = table + lax.dot_general(
            member, piece.astype(BF16), (((0,), (0,)), ((), ())), preferred_element_type=F32
        )
    per = counts.shape[0]
    for i in range(per):
        hit = (jnp.broadcast_to(ids, (nall, lanes)) == me * per + i).astype(F32)
        counts[i : i + 1, :] = jnp.sum(hit, 0, keepdims=True)
    E[0:lanes, :] = table
    scaled = constants[0 : high.shape[1], :]
    for j in range(nlat):
        value = scaled * E[j : j + 1, :]
        upper = value.astype(BF16)
        high[j] = upper
        low[j] = (value - upper.astype(F32)).astype(BF16)


def times(a, b):
    return lax.dot_general(a, b, (((1,), (1,)), ((), ())), preferred_element_type=F32)


def split(value):
    upper = value.astype(BF16)
    return upper, (value - upper.astype(F32)).astype(BF16)


def spread_kernel(high, low, last, own, sends):
    nlat, nproj, nchan = high.shape
    ndev, per, width = sends.shape
    top, rest = split(last[...])
    rows = 256
    for r in range(0, nlat * nproj, rows):
        upper = high[r // nproj : (r + rows) // nproj].reshape(rows, nchan)
        lower = low[r // nproj : (r + rows) // nproj].reshape(rows, nchan)
        z = times(upper, top) + times(upper, rest) + times(lower, top)
        sends[r // per : (r + rows) // per] = z.reshape(rows // per, per, width).astype(BF16)
    me = lax.axis_index("tm")

    @pl.when(me < ndev - 1)
    def _():
        block = sends[me + 1]
        moved = own[2 * nproj : 3 * nproj, :]
        sends[me + 1, 0:nproj] = (block[0:nproj].astype(F32) + moved).astype(BF16)


def conv_kernel(
    window, packing, x_hbm, halo_hbm, mine, da, db, dc, so, sa, sb, sc, constants,
    feat_hbm, last, sums, w, X, HA, HB, FA, FB, R, pooled, kept, wsem, insem, outsem, *, shards,
):
    nframe, npos, nchan = x_hbm.shape
    tiles, groups = npos // TILE, nframe // GROUP
    total = tiles * groups
    H, F = (HA, HB), (FA, FB)
    half = da.shape[1]
    depth = 2 * half
    nproj = sums.shape[0] // 3
    me = lax.axis_index("dp")
    side = lax.rem(lax.axis_index("tm"), 2)
    lead = KT - 1

    def weights():
        copies = []
        slot = 0
        for step, near, far in ((0, mine, so), (shards - 1, da, sa), (1, db, sb), (2, dc, sc)):
            base = lax.rem(me + step, shards) * depth
            for piece, lane in ((near, side), (far, 1 - side)):
                row = pl.multiple_of(base + lane * half, half)
                copies.append(pltpu.make_async_copy(piece, w.at[:, pl.ds(row, half)], wsem.at[slot]))
                slot += 1
        return copies

    def entering(q):
        part = pl.ds(q * TILE, TILE)
        return pltpu.make_async_copy(x_hbm.at[:, part], X.at[lead : lead + nframe, part], insem.at[q])

    def prior(q):
        part = pl.ds(q * TILE, TILE)
        return pltpu.make_async_copy(halo_hbm.at[:, part], X.at[0:lead, part], insem.at[tiles + q])

    def place(i):
        if isinstance(i, int):
            return i // groups * TILE, i % groups * GROUP
        return pl.multiple_of(i // groups * TILE, TILE), lax.rem(i, groups) * GROUP

    def leaving(i, s):
        p, f = place(i)
        return pltpu.make_async_copy(F[s], feat_hbm.at[pl.ds(f, GROUP), pl.ds(p, TILE)], outsem.at[s])

    def product(i, s, m, n):
        p, f = place(i)
        count = ROWS // TILE
        acc = None
        for k in range(KT):
            rows = X[pl.ds(f + lead - k + m * count, count), pl.ds(p, TILE), :].reshape(ROWS, nchan)
            part = jnp.dot(rows, w[k, :, n : n + 256], preferred_element_type=F32)
            acc = part if acc is None else acc + part
        H[s][m * ROWS : (m + 1) * ROWS, n : n + 256] = acc

    def activate(i, s, g, r):
        p, f = place(i)
        at = g * TILE + r
        h = H[s][at : at + SUB, :]
        c = X[f + lead + g, pl.ds(p + r, SUB), :].astype(F32)
        value = c + (h + h * jnp.tanh(h))
        F[s][g, r : r + SUB, :] = value.astype(BF16)
        mean = jnp.sum(value * value, -1, keepdims=True) * (1.0 / nchan)
        R[at : at + SUB, :] = jnp.broadcast_to(lax.rsqrt(mean + 1e-06), (SUB, 128))

    def recur(i, s, r):
        p, f = place(i)
        rows = pl.ds(p + r, SUB)
        state = last[rows, :]
        for g in range(GROUP):
            scale = R[g * TILE + r : g * TILE + r + SUB, :]
            v = F[s][g, r : r + SUB, :].astype(F32)
            v = jnp.concatenate([v[:, n : n + 128] * scale for n in range(0, nchan, 128)], 1)
            state = state * kept[pl.ds(f + g, 1), :] + v
            pooled[window[f + g], rows, :] += state
        last[rows, :] = state

    products = [(m, n) for m in range(GROUP * TILE // ROWS) for n in range(0, nchan, 256)]

    def project(q):
        part = slice(q * TILE, (q + 1) * TILE)
        upper, lower = split(constants[0:nproj, :])
        both = jnp.concatenate([upper, lower], 0)
        for j in range(3):
            top, rest = split(pooled[j, part, :])
            value = times(both, top)
            sums[j * nproj : (j + 1) * nproj, part] = value[:nproj] + value[nproj:] + times(upper, rest)

    def stage(later, ls, i, s):
        work = [(g, r) for r in range(0, TILE, SUB) for g in range(GROUP)] + [(None, r) for r in range(0, TILE, SUB)]
        todo = [] if later is None else list(products)
        for at, (g, r) in enumerate(work):
            if todo and at * len(products) // len(work) >= len(products) - len(todo):
                product(later, ls, *todo.pop(0))
            if g is None:
                recur(i, s, r)
            else:
                activate(i, s, g, r)

    pieces = weights()
    for copy in pieces:
        copy.start()
    for q in range(tiles):
        prior(q).start()
        entering(q).start()
    kept[...] = constants[nproj : nproj + 1, :] * packing[:, 0:1]
    last[...] = jnp.zeros_like(last)
    pooled[...] = jnp.zeros_like(pooled)
    for copy in pieces:
        copy.wait()
    prior(0).wait()
    entering(0).wait()
    for m, n in products:
        product(0, 0, m, n)

    def body(step, _):
        i = 2 * step

        @pl.when(step > 0)
        def _():
            leaving(i - 2, 0).wait()
            leaving(i - 1, 1).wait()

        stage(i + 1, 1, i, 0)
        leaving(i, 0).start()
        q = (i + 2) // groups

        @pl.when(jnp.logical_and(lax.rem(i + 2, groups) == 0, q < tiles))
        def _():
            prior(q).wait()
            entering(q).wait()

        stage(i + 2, 0, i + 1, 1)
        leaving(i + 1, 1).start()
        return 0

    lax.fori_loop(0, total // 2 - 1, body, 0)
    leaving(total - 4, 0).wait()
    leaving(total - 3, 1).wait()
    stage(total - 1, 1, total - 2, 0)
    leaving(total - 2, 0).start()
    for q in range(tiles - 1):
        project(q)
    stage(None, None, total - 1, 1)
    leaving(total - 1, 1).start()
    project(tiles - 1)
    leaving(total - 2, 0).wait()
    leaving(total - 1, 1).wait()


def final_kernel(counts, *refs):
    per = counts.shape[0]
    latents = refs[-1]
    start = 0
    for index in range(len(refs) // 2):
        got, own = refs[2 * index], refs[2 * index + 1]
        ndev, rows, width = got.shape
        nproj = rows // per
        for i in range(per):
            part = slice(i * nproj, (i + 1) * nproj)
            total = own[part, :]
            for d in range(ndev):
                total = total + got[d, part, :].astype(F32)
            for n in range(0, width, 128):
                latents[i, :, start + n : start + n + 128] = total[:, n : n + 128] / counts[i : i + 1, :]
        start += width


def per_device(clips, w_time, gain, rate, keep, latent_ids, w_lat):
    _, nframe, npos, nchan = clips.shape
    nproj = w_lat.shape[1]
    ndev = lax.axis_size("tm")
    shards = lax.axis_size("dp")
    nall = nframe * ndev
    per = nframe // STRIDE
    nlat = per * ndev
    me = lax.axis_index("tm")
    side = me % 2
    x = clips[0]

    half = w_time.shape[1] // 2
    mine = lax.dynamic_slice_in_dim(w_time, side * half, half, 1) * jnp.asarray(0.5, BF16)
    dc = rotated(mine, "dp", 2)
    da = rotated(mine, "dp", 1)
    db = rotated(mine, "dp", -1)
    so = swapped(mine, "tm")
    sa, sb, sc = swapped(da, "tm"), swapped(db, "tm"), swapped(dc, "tm")
    rate, gain, w_lat, _ = lax.optimization_barrier((rate, gain, w_lat, mine))
    halo = shifted(x[nframe - (KT - 1) :], "tm", 1)
    window = latent_ids - me.astype(jnp.int32) * per
    lane = jnp.arange(128, dtype=jnp.int32)[None]
    packing = jnp.where(lane < 64, keep[:, None], latent_ids.astype(F32)[:, None])
    local = jnp.broadcast_to(packing[None], (ndev, nframe, 128))
    packed = lax.all_to_all(local, "tm", 0, 0).reshape(nall, 128)

    inject = jnp.sqrt(-jnp.expm1(-2.0 * rate))
    row = jnp.arange(nproj + 8, dtype=jnp.int32)[:, None]
    padded = jnp.pad(w_lat.T.astype(F32), ((0, 8), (0, 0)))
    constants = jnp.where(row < nproj, padded * (inject * gain)[None], jnp.exp(-rate)[None])

    vmem = pl.BlockSpec(memory_space=pltpu.VMEM)
    smem = pl.BlockSpec(memory_space=pltpu.SMEM)
    hbm = pl.BlockSpec(memory_space=pltpu.HBM)
    table_shape = jax.ShapeDtypeStruct((nlat, nproj, nchan), BF16)

    stage_rows = GROUP * TILE
    conv = pl.pallas_call(
        functools.partial(conv_kernel, shards=shards),
        out_shape=(
            jax.ShapeDtypeStruct((nframe, npos, nchan), BF16),
            jax.ShapeDtypeStruct((npos, nchan), F32),
            jax.ShapeDtypeStruct((3 * nproj, npos), F32),
        ),
        in_specs=[smem, vmem] + [hbm] * 10 + [vmem],
        out_specs=(hbm, vmem, vmem),
        scratch_shapes=[
            pltpu.VMEM((KT, nchan, nchan), BF16),
            pltpu.VMEM((nframe + KT - 1, npos, nchan), BF16),
            pltpu.VMEM((stage_rows, nchan), F32),
            pltpu.VMEM((stage_rows, nchan), F32),
            pltpu.VMEM((GROUP, TILE, nchan), BF16),
            pltpu.VMEM((GROUP, TILE, nchan), BF16),
            pltpu.VMEM((stage_rows, 128), F32),
            pltpu.VMEM((3, npos, nchan), F32),
            pltpu.VMEM((nframe, nchan), F32),
            pltpu.SemaphoreType.DMA((8,)),
            pltpu.SemaphoreType.DMA((2 * npos // TILE,)),
            pltpu.SemaphoreType.DMA((2,)),
        ],
        compiler_params=pltpu.CompilerParams(vmem_limit_bytes=48 << 20),
        cost_estimate=pl.CostEstimate(
            flops=2 * KT * nframe * npos * nchan * nchan,
            bytes_accessed=4 * nframe * npos * nchan,
            transcendentals=nframe * npos * nchan,
        ),
        name="conv",
    )
    features, last, own = conv(window, packing, x, halo, mine, da, db, dc, so, sa, sb, sc, constants)
    packed, last = lax.optimization_barrier((packed, last))
    high, low, counts = pl.pallas_call(
        table_kernel,
        out_shape=(table_shape, table_shape, jax.ShapeDtypeStruct((per, 128), F32)),
        in_specs=[vmem] * 3,
        out_specs=(vmem,) * 3,
        scratch_shapes=[pltpu.VMEM((nall, nchan), F32)],
        compiler_params=pltpu.CompilerParams(vmem_limit_bytes=16 << 20),
        cost_estimate=pl.CostEstimate(
            flops=12 * nlat * nall * nchan, bytes_accessed=4 << 20, transcendentals=nall * nchan
        ),
        name="tables",
    )(packed, rate[None], constants)
    sends = pl.pallas_call(
        spread_kernel,
        out_shape=jax.ShapeDtypeStruct((ndev, per * nproj, npos), BF16),
        in_specs=[vmem] * 4,
        out_specs=vmem,
        compiler_params=pltpu.CompilerParams(vmem_limit_bytes=16 << 20),
        name="spread",
    )(high, low, last, own)
    outs = [lax.all_to_all(sends, "tm", 0, 0), own]
    latents = pl.pallas_call(
        final_kernel,
        out_shape=jax.ShapeDtypeStruct((per, nproj, npos), F32),
        in_specs=[vmem] * (1 + len(outs)),
        out_specs=vmem,
        compiler_params=pltpu.CompilerParams(vmem_limit_bytes=16 << 20),
        name="final",
    )(counts, *outs)
    return features[None], latents[None]


def solution(mesh):
    return jax.shard_map(
        per_device,
        mesh=mesh,
        in_specs=(P("dp", "tm", None, None), P(None, "dp", None), P(), P(), P("tm"), P("tm"), P()),
        out_specs=(P("dp", "tm", None, None), P("dp", "tm", None, None)),
        check_vma=False,
    )
```

```python
import functools

import jax
import jax.numpy as jnp
from jax import lax
from jax.experimental import pallas as pl
from jax.experimental.pallas import tpu as pltpu
from jax.sharding import PartitionSpec as P


KT = 3
STRIDE = 8
F32 = jnp.float32
BF16 = jnp.bfloat16
TILE = 128
GROUP = 4
ROWS = 256
SUB = 16


def rotated(value, axis, steps):
    count = lax.axis_size(axis)
    return lax.ppermute(value, axis, [(s, (s + steps) % count) for s in range(count)])


def shifted(value, axis, steps):
    count = lax.axis_size(axis)
    return lax.ppermute(value, axis, [(s, s + steps) for s in range(count - steps)])


def swapped(value, axis):
    return lax.ppermute(value, axis, [(s, s ^ 1) for s in range(lax.axis_size(axis))])


def pieces_of(value):
    one = value.astype(BF16).astype(F32)
    two = (value - one).astype(BF16).astype(F32)
    return one, two, value - one - two


def times(a, b):
    return lax.dot_general(a, b, (((1,), (1,)), ((), ())), preferred_element_type=F32)


def split(value):
    upper = value.astype(BF16)
    return upper, (value - upper.astype(F32)).astype(BF16)


def spread_kernel(packed, rate, constants, last, own, sends, counts, E):
    nall, lanes = packed.shape
    nchan = rate.shape[1]
    ndev, per, width = sends.shape
    nproj = own.shape[0] // 3
    nlat = ndev * per // nproj
    me = lax.axis_index("tm")
    end = (me + 1) * (nall // lax.axis_size("tm")) - 1
    frame = lax.broadcasted_iota(jnp.int32, (nall, lanes), 0)
    lane = lax.broadcasted_iota(jnp.int32, (nall, lanes), 1)
    logs = jnp.where(frame > end, jnp.log(packed[:, 0:1]), 0.0)
    one, two, three = pieces_of(logs)
    pieces = jnp.where(lane == 0, one, jnp.where(lane == 1, two, jnp.where(lane == 2, three, 0.0)))
    rows = lax.broadcasted_iota(jnp.int32, (nall, nall), 0)
    cols = lax.broadcasted_iota(jnp.int32, (nall, nall), 1)
    lower = jnp.where(cols <= rows, 1.0, 0.0).astype(BF16)
    run = jnp.dot(lower, pieces.astype(BF16), preferred_element_type=F32)
    run = jnp.sum(run, -1, keepdims=True)
    block = 128
    for r in range(0, nall, block):
        at = lax.broadcasted_iota(jnp.int32, (block, nchan), 0) + r
        gap = (at - end).astype(F32)
        E[r : r + block, :] = jnp.where(at > end, jnp.exp(run[r : r + block] - rate[...] * gap), 0.0)
    ids = packed[:, lanes // 2 : lanes // 2 + 1].astype(jnp.int32)
    member = jnp.where(lane == ids, 1.0, 0.0).astype(BF16)
    table = jnp.zeros((lanes, nchan), F32)
    for piece in pieces_of(E[...]):
        table = table + lax.dot_general(
            member, piece.astype(BF16), (((0,), (0,)), ((), ())), preferred_element_type=F32
        )
    for i in range(counts.shape[0]):
        hit = (jnp.broadcast_to(ids, (nall, lanes)) == me * counts.shape[0] + i).astype(F32)
        counts[i : i + 1, :] = jnp.sum(hit, 0, keepdims=True)
    E[0:lanes, :] = table
    scaled = constants[0:nproj, :]
    top, rest = split(last[...])
    rows = 256
    group = rows // nproj
    for r in range(0, nlat, group):
        value = jnp.concatenate([scaled * E[j : j + 1, :] for j in range(r, r + group)], 0)
        upper, lower = split(value)
        z = times(jnp.concatenate([upper, lower], 0), top)
        z = z[:rows] + z[rows:] + times(upper, rest)
        first = r * nproj // per
        sends[first : first + rows // per] = z.reshape(rows // per, per, width).astype(BF16)

    @pl.when(me < ndev - 1)
    def _():
        block = sends[me + 1]
        moved = own[2 * nproj : 3 * nproj, :]
        sends[me + 1, 0:nproj] = (block[0:nproj].astype(F32) + moved).astype(BF16)


def conv_kernel(
    window, packing, x_hbm, halo_hbm, mine, da, db, dc, so, sa, sb, sc, constants,
    feat_hbm, last, sums, w, X, HA, HB, FA, FB, R, pooled, kept, wsem, insem, outsem, *, shards,
):
    nframe, npos, nchan = x_hbm.shape
    tiles, groups = npos // TILE, nframe // GROUP
    total = tiles * groups
    H, F = (HA, HB), (FA, FB)
    half = da.shape[1]
    depth = 2 * half
    nproj = sums.shape[0] // 3
    me = lax.axis_index("dp")
    side = lax.rem(lax.axis_index("tm"), 2)
    lead = KT - 1

    def weights():
        copies = []
        slot = 0
        for step, near, far in ((0, mine, so), (shards - 1, da, sa), (1, db, sb), (2, dc, sc)):
            base = lax.rem(me + step, shards) * depth
            for piece, lane in ((near, side), (far, 1 - side)):
                row = pl.multiple_of(base + lane * half, half)
                copies.append(pltpu.make_async_copy(piece, w.at[:, pl.ds(row, half)], wsem.at[slot]))
                slot += 1
        return copies

    def entering(q):
        part = pl.ds(q * TILE, TILE)
        return pltpu.make_async_copy(x_hbm.at[:, part], X.at[lead : lead + nframe, part], insem.at[q])

    def prior(q):
        part = pl.ds(q * TILE, TILE)
        return pltpu.make_async_copy(halo_hbm.at[:, part], X.at[0:lead, part], insem.at[tiles + q])

    def place(i):
        if isinstance(i, int):
            return i // groups * TILE, i % groups * GROUP
        return pl.multiple_of(i // groups * TILE, TILE), lax.rem(i, groups) * GROUP

    def leaving(i, s):
        p, f = place(i)
        return pltpu.make_async_copy(F[s], feat_hbm.at[pl.ds(f, GROUP), pl.ds(p, TILE)], outsem.at[s])

    def product(i, s, m, n):
        p, f = place(i)
        count = ROWS // TILE
        acc = None
        for k in range(KT):
            rows = X[pl.ds(f + lead - k + m * count, count), pl.ds(p, TILE), :].reshape(ROWS, nchan)
            part = jnp.dot(rows, w[k, :, n : n + 256], preferred_element_type=F32)
            acc = part if acc is None else acc + part
        H[s][m * ROWS : (m + 1) * ROWS, n : n + 256] = acc

    def activate(i, s, g, r):
        p, f = place(i)
        at = g * TILE + r
        h = H[s][at : at + SUB, :]
        c = X[f + lead + g, pl.ds(p + r, SUB), :].astype(F32)
        value = c + (h + h * jnp.tanh(h))
        F[s][g, r : r + SUB, :] = value.astype(BF16)
        mean = jnp.sum(value * value, -1, keepdims=True) * (1.0 / nchan)
        R[at : at + SUB, :] = jnp.broadcast_to(lax.rsqrt(mean + 1e-06), (SUB, 128))

    def recur(i, s, r):
        p, f = place(i)
        rows = pl.ds(p + r, SUB)
        state = last[rows, :]
        for g in range(GROUP):
            scale = R[g * TILE + r : g * TILE + r + SUB, :]
            v = F[s][g, r : r + SUB, :].astype(F32)
            v = jnp.concatenate([v[:, n : n + 128] * scale for n in range(0, nchan, 128)], 1)
            state = state * kept[pl.ds(f + g, 1), :] + v
            pooled[window[f + g], rows, :] += state
        last[rows, :] = state

    products = [(m, n) for m in range(GROUP * TILE // ROWS) for n in range(0, nchan, 256)]

    def project(q):
        part = slice(q * TILE, (q + 1) * TILE)
        upper, lower = split(constants[0:nproj, :])
        both = jnp.concatenate([upper, lower], 0)
        for j in range(3):
            top, rest = split(pooled[j, part, :])
            value = times(both, top)
            sums[j * nproj : (j + 1) * nproj, part] = value[:nproj] + value[nproj:] + times(upper, rest)

    def stage(later, ls, i, s):
        work = [(g, r) for r in range(0, TILE, SUB) for g in range(GROUP)] + [(None, r) for r in range(0, TILE, SUB)]
        todo = [] if later is None else list(products)
        for at, (g, r) in enumerate(work):
            if todo and at * len(products) // len(work) >= len(products) - len(todo):
                product(later, ls, *todo.pop(0))
            if g is None:
                recur(i, s, r)
            else:
                activate(i, s, g, r)

    pieces = weights()
    for copy in pieces:
        copy.start()
    for q in range(tiles):
        prior(q).start()
        entering(q).start()
    kept[...] = constants[nproj : nproj + 1, :] * packing[:, 0:1]
    last[...] = jnp.zeros_like(last)
    pooled[...] = jnp.zeros_like(pooled)
    for copy in pieces:
        copy.wait()
    prior(0).wait()
    entering(0).wait()
    for m, n in products:
        product(0, 0, m, n)

    def body(step, _):
        i = 2 * step

        @pl.when(step > 0)
        def _():
            leaving(i - 2, 0).wait()
            leaving(i - 1, 1).wait()

        stage(i + 1, 1, i, 0)
        leaving(i, 0).start()
        q = (i + 2) // groups

        @pl.when(jnp.logical_and(lax.rem(i + 2, groups) == 0, q < tiles))
        def _():
            prior(q).wait()
            entering(q).wait()

        stage(i + 2, 0, i + 1, 1)
        leaving(i + 1, 1).start()
        return 0

    lax.fori_loop(0, total // 2 - 1, body, 0)
    leaving(total - 4, 0).wait()
    leaving(total - 3, 1).wait()
    stage(total - 1, 1, total - 2, 0)
    leaving(total - 2, 0).start()
    for q in range(tiles - 1):
        project(q)
    stage(None, None, total - 1, 1)
    leaving(total - 1, 1).start()
    project(tiles - 1)
    leaving(total - 2, 0).wait()
    leaving(total - 1, 1).wait()


def final_kernel(counts, *refs):
    per = counts.shape[0]
    latents = refs[-1]
    start = 0
    for index in range(len(refs) // 2):
        got, own = refs[2 * index], refs[2 * index + 1]
        ndev, rows, width = got.shape
        nproj = rows // per
        for i in range(per):
            part = slice(i * nproj, (i + 1) * nproj)
            total = own[part, :]
            for d in range(ndev):
                total = total + got[d, part, :].astype(F32)
            for n in range(0, width, 128):
                latents[i, :, start + n : start + n + 128] = total[:, n : n + 128] / counts[i : i + 1, :]
        start += width


def per_device(clips, w_time, gain, rate, keep, latent_ids, w_lat):
    _, nframe, npos, nchan = clips.shape
    nproj = w_lat.shape[1]
    ndev = lax.axis_size("tm")
    shards = lax.axis_size("dp")
    nall = nframe * ndev
    per = nframe // STRIDE
    me = lax.axis_index("tm")
    side = me % 2
    x = clips[0]

    half = w_time.shape[1] // 2
    mine = lax.dynamic_slice_in_dim(w_time, side * half, half, 1) * jnp.asarray(0.5, BF16)
    dc = rotated(mine, "dp", 2)
    da = rotated(mine, "dp", 1)
    db = rotated(mine, "dp", -1)
    so = swapped(mine, "tm")
    sa, sb, sc = swapped(da, "tm"), swapped(db, "tm"), swapped(dc, "tm")
    rate, gain, w_lat, _ = lax.optimization_barrier((rate, gain, w_lat, mine))
    halo = shifted(x[nframe - (KT - 1) :], "tm", 1)
    window = latent_ids - me.astype(jnp.int32) * per
    lane = jnp.arange(128, dtype=jnp.int32)[None]
    packing = jnp.where(lane < 64, keep[:, None], latent_ids.astype(F32)[:, None])
    local = jnp.broadcast_to(packing[None], (ndev, nframe, 128))
    packed = lax.all_to_all(local, "tm", 0, 0).reshape(nall, 128)

    inject = jnp.sqrt(-jnp.expm1(-2.0 * rate))
    row = jnp.arange(nproj + 8, dtype=jnp.int32)[:, None]
    padded = jnp.pad(w_lat.T.astype(F32), ((0, 8), (0, 0)))
    constants = jnp.where(row < nproj, padded * (inject * gain)[None], jnp.exp(-rate)[None])

    vmem = pl.BlockSpec(memory_space=pltpu.VMEM)
    smem = pl.BlockSpec(memory_space=pltpu.SMEM)
    hbm = pl.BlockSpec(memory_space=pltpu.HBM)

    stage_rows = GROUP * TILE
    conv = pl.pallas_call(
        functools.partial(conv_kernel, shards=shards),
        out_shape=(
            jax.ShapeDtypeStruct((nframe, npos, nchan), BF16),
            jax.ShapeDtypeStruct((npos, nchan), F32),
            jax.ShapeDtypeStruct((3 * nproj, npos), F32),
        ),
        in_specs=[smem, vmem] + [hbm] * 10 + [vmem],
        out_specs=(hbm, vmem, vmem),
        scratch_shapes=[
            pltpu.VMEM((KT, nchan, nchan), BF16),
            pltpu.VMEM((nframe + KT - 1, npos, nchan), BF16),
            pltpu.VMEM((stage_rows, nchan), F32),
            pltpu.VMEM((stage_rows, nchan), F32),
            pltpu.VMEM((GROUP, TILE, nchan), BF16),
            pltpu.VMEM((GROUP, TILE, nchan), BF16),
            pltpu.VMEM((stage_rows, 128), F32),
            pltpu.VMEM((3, npos, nchan), F32),
            pltpu.VMEM((nframe, nchan), F32),
            pltpu.SemaphoreType.DMA((8,)),
            pltpu.SemaphoreType.DMA((2 * npos // TILE,)),
            pltpu.SemaphoreType.DMA((2,)),
        ],
        compiler_params=pltpu.CompilerParams(vmem_limit_bytes=48 << 20),
        cost_estimate=pl.CostEstimate(
            flops=2 * KT * nframe * npos * nchan * nchan,
            bytes_accessed=4 * nframe * npos * nchan,
            transcendentals=nframe * npos * nchan,
        ),
        name="conv",
    )
    features, last, own = conv(window, packing, x, halo, mine, da, db, dc, so, sa, sb, sc, constants)
    packed, last = lax.optimization_barrier((packed, last))
    sends, counts = pl.pallas_call(
        spread_kernel,
        out_shape=(
            jax.ShapeDtypeStruct((ndev, per * nproj, npos), BF16),
            jax.ShapeDtypeStruct((per, 128), F32),
        ),
        in_specs=[vmem] * 5,
        out_specs=(vmem,) * 2,
        scratch_shapes=[pltpu.VMEM((nall, nchan), F32)],
        compiler_params=pltpu.CompilerParams(vmem_limit_bytes=16 << 20),
        name="spread",
    )(packed, rate[None], constants, last, own)
    outs = [lax.all_to_all(sends, "tm", 0, 0), own]
    latents = pl.pallas_call(
        final_kernel,
        out_shape=jax.ShapeDtypeStruct((per, nproj, npos), F32),
        in_specs=[vmem] * (1 + len(outs)),
        out_specs=vmem,
        compiler_params=pltpu.CompilerParams(vmem_limit_bytes=16 << 20),
        name="final",
    )(counts, *outs)
    return features[None], latents[None]


def solution(mesh):
    return jax.shard_map(
        per_device,
        mesh=mesh,
        in_specs=(P("dp", "tm", None, None), P(None, "dp", None), P(), P(), P("tm"), P("tm"), P()),
        out_specs=(P("dp", "tm", None, None), P("dp", "tm", None, None)),
        check_vma=False,
    )
```

```python
import functools

import jax
import jax.numpy as jnp
from jax import lax
from jax.experimental import pallas as pl
from jax.experimental.pallas import tpu as pltpu
from jax.sharding import PartitionSpec as P


KT = 3
STRIDE = 8
F32 = jnp.float32
BF16 = jnp.bfloat16
TILE = 128
GROUP = 4
ROWS = 256
SUB = 16


def rotated(value, axis, steps):
    count = lax.axis_size(axis)
    return lax.ppermute(value, axis, [(s, (s + steps) % count) for s in range(count)])


def shifted(value, axis, steps):
    count = lax.axis_size(axis)
    return lax.ppermute(value, axis, [(s, s + steps) for s in range(count - steps)])


def swapped(value, axis):
    return lax.ppermute(value, axis, [(s, s ^ 1) for s in range(lax.axis_size(axis))])


def pieces_of(value):
    one = value.astype(BF16).astype(F32)
    two = (value - one).astype(BF16).astype(F32)
    return one, two, value - one - two


def times(a, b):
    return lax.dot_general(a, b, (((1,), (1,)), ((), ())), preferred_element_type=F32)


def split(value):
    upper = value.astype(BF16)
    return upper, (value - upper.astype(F32)).astype(BF16)


def spread_kernel(packed, rate, constants, last, own, sends, counts, E):
    nall, lanes = packed.shape
    nchan = rate.shape[1]
    ndev, per, width = sends.shape
    nproj = own.shape[0] // 3
    nlat = ndev * per // nproj
    me = lax.axis_index("tm")
    end = (me + 1) * (nall // lax.axis_size("tm")) - 1
    frame = lax.broadcasted_iota(jnp.int32, (nall, lanes), 0)
    lane = lax.broadcasted_iota(jnp.int32, (nall, lanes), 1)
    logs = jnp.where(frame > end, jnp.log(packed[:, 0:1]), 0.0)
    one, two, three = pieces_of(logs)
    pieces = jnp.where(lane == 0, one, jnp.where(lane == 1, two, jnp.where(lane == 2, three, 0.0)))
    rows = lax.broadcasted_iota(jnp.int32, (nall, nall), 0)
    cols = lax.broadcasted_iota(jnp.int32, (nall, nall), 1)
    lower = jnp.where(cols <= rows, 1.0, 0.0).astype(BF16)
    run = jnp.dot(lower, pieces.astype(BF16), preferred_element_type=F32)
    run = jnp.sum(run, -1, keepdims=True)
    block = 128
    for r in range(0, nall, block):
        at = lax.broadcasted_iota(jnp.int32, (block, nchan), 0) + r
        gap = (at - end).astype(F32)
        E[r : r + block, :] = jnp.where(at > end, jnp.exp(run[r : r + block] - rate[...] * gap), 0.0)
    ids = packed[:, lanes // 2 : lanes // 2 + 1].astype(jnp.int32)
    member = jnp.where(lane == ids, 1.0, 0.0).astype(BF16)
    table = jnp.zeros((lanes, nchan), F32)
    for piece in pieces_of(E[...]):
        table = table + lax.dot_general(
            member, piece.astype(BF16), (((0,), (0,)), ((), ())), preferred_element_type=F32
        )
    for i in range(counts.shape[0]):
        hit = (jnp.broadcast_to(ids, (nall, lanes)) == me * counts.shape[0] + i).astype(F32)
        counts[i : i + 1, :] = jnp.sum(hit, 0, keepdims=True)
    E[0:lanes, :] = table
    scaled = constants[0:nproj, :]
    top, rest = split(last[...])
    rows = 256
    group = rows // nproj
    for r in range(0, nlat, group):
        value = jnp.concatenate([scaled * E[j : j + 1, :] for j in range(r, r + group)], 0)
        upper, lower = split(value)
        z = times(upper, top) + times(upper, rest) + times(lower, top)
        first = r * nproj // per
        sends[first : first + rows // per] = z.reshape(rows // per, per, width).astype(BF16)

    @pl.when(me < ndev - 1)
    def _():
        block = sends[me + 1]
        moved = own[2 * nproj : 3 * nproj, :]
        sends[me + 1, 0:nproj] = (block[0:nproj].astype(F32) + moved).astype(BF16)


def conv_kernel(
    window, local, x_hbm, halo_hbm, mine, da, db, dc, so, sa, sb, sc, constants,
    feat_hbm, last, sums, w, X, HA, HB, FA, FB, R, pooled, kept, packing, wsem, insem, outsem, *, shards,
):
    nframe, npos, nchan = x_hbm.shape
    tiles, groups = npos // TILE, nframe // GROUP
    total = tiles * groups
    H, F = (HA, HB), (FA, FB)
    half = da.shape[1]
    depth = 2 * half
    nproj = sums.shape[0] // 3
    me = lax.axis_index("dp")
    side = lax.rem(lax.axis_index("tm"), 2)
    lead = KT - 1

    def weights():
        copies = []
        slot = 0
        for step, near, far in ((0, mine, so), (shards - 1, da, sa), (1, db, sb), (2, dc, sc)):
            base = lax.rem(me + step, shards) * depth
            for piece, lane in ((near, side), (far, 1 - side)):
                row = pl.multiple_of(base + lane * half, half)
                copies.append(pltpu.make_async_copy(piece, w.at[:, pl.ds(row, half)], wsem.at[slot]))
                slot += 1
        return copies

    def entering(q):
        part = pl.ds(q * TILE, TILE)
        return pltpu.make_async_copy(x_hbm.at[:, part], X.at[lead : lead + nframe, part], insem.at[q])

    def prior(q):
        part = pl.ds(q * TILE, TILE)
        return pltpu.make_async_copy(halo_hbm.at[:, part], X.at[0:lead, part], insem.at[tiles + q])

    def place(i):
        if isinstance(i, int):
            return i // groups * TILE, i % groups * GROUP
        return pl.multiple_of(i // groups * TILE, TILE), lax.rem(i, groups) * GROUP

    def leaving(i, s):
        p, f = place(i)
        return pltpu.make_async_copy(F[s], feat_hbm.at[pl.ds(f, GROUP), pl.ds(p, TILE)], outsem.at[s])

    def product(i, s, m, n):
        p, f = place(i)
        count = ROWS // TILE
        acc = None
        for k in range(KT):
            rows = X[pl.ds(f + lead - k + m * count, count), pl.ds(p, TILE), :].reshape(ROWS, nchan)
            part = jnp.dot(rows, w[k, :, n : n + 256], preferred_element_type=F32)
            acc = part if acc is None else acc + part
        H[s][m * ROWS : (m + 1) * ROWS, n : n + 256] = acc

    def activate(i, s, g, r):
        p, f = place(i)
        at = g * TILE + r
        h = H[s][at : at + SUB, :]
        c = X[f + lead + g, pl.ds(p + r, SUB), :].astype(F32)
        value = c + (h + h * jnp.tanh(h))
        F[s][g, r : r + SUB, :] = value.astype(BF16)
        mean = jnp.sum(value * value, -1, keepdims=True) * (1.0 / nchan)
        R[at : at + SUB, :] = jnp.broadcast_to(lax.rsqrt(mean + 1e-06), (SUB, 128))

    def recur(i, s, r):
        p, f = place(i)
        rows = pl.ds(p + r, SUB)
        state = last[rows, :]
        for g in range(GROUP):
            scale = R[g * TILE + r : g * TILE + r + SUB, :]
            v = F[s][g, r : r + SUB, :].astype(F32)
            v = jnp.concatenate([v[:, n : n + 128] * scale for n in range(0, nchan, 128)], 1)
            state = state * kept[pl.ds(f + g, 1), :] + v
            pooled[window[f + g], rows, :] += state
        last[rows, :] = state

    products = [(m, n) for m in range(GROUP * TILE // ROWS) for n in range(0, nchan, 256)]

    def project(q):
        part = slice(q * TILE, (q + 1) * TILE)
        upper, lower = split(constants[0:nproj, :])
        both = jnp.concatenate([upper, lower], 0)
        for j in range(3):
            top, rest = split(pooled[j, part, :])
            value = times(both, top)
            sums[j * nproj : (j + 1) * nproj, part] = value[:nproj] + value[nproj:] + times(upper, rest)

    def stage(later, ls, i, s):
        work = [(g, r) for r in range(0, TILE, SUB) for g in range(GROUP)] + [(None, r) for r in range(0, TILE, SUB)]
        todo = [] if later is None else list(products)
        for at, (g, r) in enumerate(work):
            if todo and at * len(products) // len(work) >= len(products) - len(todo):
                product(later, ls, *todo.pop(0))
            if g is None:
                recur(i, s, r)
            else:
                activate(i, s, g, r)

    pieces = weights() + [pltpu.make_async_copy(local.at[0], packing, wsem.at[8])]
    for copy in pieces:
        copy.start()
    for q in range(tiles):
        prior(q).start()
        entering(q).start()
    last[...] = jnp.zeros_like(last)
    pooled[...] = jnp.zeros_like(pooled)
    for copy in pieces:
        copy.wait()
    kept[...] = constants[nproj : nproj + 1, :] * packing[:, 0:1]
    prior(0).wait()
    entering(0).wait()
    for m, n in products:
        product(0, 0, m, n)

    def body(step, _):
        i = 2 * step

        @pl.when(step > 0)
        def _():
            leaving(i - 2, 0).wait()
            leaving(i - 1, 1).wait()

        stage(i + 1, 1, i, 0)
        leaving(i, 0).start()
        q = (i + 2) // groups

        @pl.when(jnp.logical_and(lax.rem(i + 2, groups) == 0, q < tiles))
        def _():
            prior(q).wait()
            entering(q).wait()

        stage(i + 2, 0, i + 1, 1)
        leaving(i + 1, 1).start()
        return 0

    lax.fori_loop(0, total // 2 - 1, body, 0)
    leaving(total - 4, 0).wait()
    leaving(total - 3, 1).wait()
    stage(total - 1, 1, total - 2, 0)
    leaving(total - 2, 0).start()
    for q in range(tiles - 1):
        project(q)
    stage(None, None, total - 1, 1)
    leaving(total - 1, 1).start()
    project(tiles - 1)
    leaving(total - 2, 0).wait()
    leaving(total - 1, 1).wait()


def final_kernel(counts, *refs):
    per = counts.shape[0]
    latents = refs[-1]
    start = 0
    for index in range(len(refs) // 2):
        got, own = refs[2 * index], refs[2 * index + 1]
        ndev, rows, width = got.shape
        nproj = rows // per
        for i in range(per):
            part = slice(i * nproj, (i + 1) * nproj)
            total = own[part, :]
            for d in range(ndev):
                total = total + got[d, part, :].astype(F32)
            for n in range(0, width, 128):
                latents[i, :, start + n : start + n + 128] = total[:, n : n + 128] / counts[i : i + 1, :]
        start += width


def per_device(clips, w_time, gain, rate, keep, latent_ids, w_lat):
    _, nframe, npos, nchan = clips.shape
    nproj = w_lat.shape[1]
    ndev = lax.axis_size("tm")
    shards = lax.axis_size("dp")
    nall = nframe * ndev
    per = nframe // STRIDE
    me = lax.axis_index("tm")
    side = me % 2
    x = clips[0]

    half = w_time.shape[1] // 2
    mine = lax.dynamic_slice_in_dim(w_time, side * half, half, 1) * jnp.asarray(0.5, BF16)
    dc = rotated(mine, "dp", 2)
    da = rotated(mine, "dp", 1)
    db = rotated(mine, "dp", -1)
    so = swapped(mine, "tm")
    sa, sb, sc = swapped(da, "tm"), swapped(db, "tm"), swapped(dc, "tm")
    rate, gain, w_lat, _ = lax.optimization_barrier((rate, gain, w_lat, mine))
    halo = shifted(x[nframe - (KT - 1) :], "tm", 1)
    window = latent_ids - me.astype(jnp.int32) * per
    shape = (ndev, nframe, 128)
    lane = lax.broadcasted_iota(jnp.int32, shape, 2) + jnp.minimum(lax.broadcasted_iota(jnp.int32, shape, 0), 0)
    local = jnp.where(lane < 64, keep[None, :, None], latent_ids.astype(F32)[None, :, None])
    packed = lax.all_to_all(local, "tm", 0, 0).reshape(nall, 128)

    inject = jnp.sqrt(-jnp.expm1(-2.0 * rate))
    row = jnp.arange(nproj + 8, dtype=jnp.int32)[:, None]
    padded = jnp.pad(w_lat.T.astype(F32), ((0, 8), (0, 0)))
    constants = jnp.where(row < nproj, padded * (inject * gain)[None], jnp.exp(-rate)[None])

    vmem = pl.BlockSpec(memory_space=pltpu.VMEM)
    smem = pl.BlockSpec(memory_space=pltpu.SMEM)
    hbm = pl.BlockSpec(memory_space=pltpu.HBM)

    stage_rows = GROUP * TILE
    conv = pl.pallas_call(
        functools.partial(conv_kernel, shards=shards),
        out_shape=(
            jax.ShapeDtypeStruct((nframe, npos, nchan), BF16),
            jax.ShapeDtypeStruct((npos, nchan), F32),
            jax.ShapeDtypeStruct((3 * nproj, npos), F32),
        ),
        in_specs=[smem] + [hbm] * 11 + [vmem],
        out_specs=(hbm, vmem, vmem),
        scratch_shapes=[
            pltpu.VMEM((KT, nchan, nchan), BF16),
            pltpu.VMEM((nframe + KT - 1, npos, nchan), BF16),
            pltpu.VMEM((stage_rows, nchan), F32),
            pltpu.VMEM((stage_rows, nchan), F32),
            pltpu.VMEM((GROUP, TILE, nchan), BF16),
            pltpu.VMEM((GROUP, TILE, nchan), BF16),
            pltpu.VMEM((stage_rows, 128), F32),
            pltpu.VMEM((3, npos, nchan), F32),
            pltpu.VMEM((nframe, nchan), F32),
            pltpu.VMEM((nframe, 128), F32),
            pltpu.SemaphoreType.DMA((9,)),
            pltpu.SemaphoreType.DMA((2 * npos // TILE,)),
            pltpu.SemaphoreType.DMA((2,)),
        ],
        compiler_params=pltpu.CompilerParams(vmem_limit_bytes=48 << 20),
        cost_estimate=pl.CostEstimate(
            flops=2 * KT * nframe * npos * nchan * nchan,
            bytes_accessed=4 * nframe * npos * nchan,
            transcendentals=nframe * npos * nchan,
        ),
        name="conv",
    )
    features, last, own = conv(window, local, x, halo, mine, da, db, dc, so, sa, sb, sc, constants)
    packed, last = lax.optimization_barrier((packed, last))
    sends, counts = pl.pallas_call(
        spread_kernel,
        out_shape=(
            jax.ShapeDtypeStruct((ndev, per * nproj, npos), BF16),
            jax.ShapeDtypeStruct((per, 128), F32),
        ),
        in_specs=[vmem] * 5,
        out_specs=(vmem,) * 2,
        scratch_shapes=[pltpu.VMEM((nall, nchan), F32)],
        compiler_params=pltpu.CompilerParams(vmem_limit_bytes=16 << 20),
        name="spread",
    )(packed, rate[None], constants, last, own)
    outs = [lax.all_to_all(sends, "tm", 0, 0), own]
    latents = pl.pallas_call(
        final_kernel,
        out_shape=jax.ShapeDtypeStruct((per, nproj, npos), F32),
        in_specs=[vmem] * (1 + len(outs)),
        out_specs=vmem,
        compiler_params=pltpu.CompilerParams(vmem_limit_bytes=16 << 20),
        name="final",
    )(counts, *outs)
    return features[None], latents[None]


def solution(mesh):
    return jax.shard_map(
        per_device,
        mesh=mesh,
        in_specs=(P("dp", "tm", None, None), P(None, "dp", None), P(), P(), P("tm"), P("tm"), P()),
        out_specs=(P("dp", "tm", None, None), P("dp", "tm", None, None)),
        check_vma=False,
    )
```
